32 devices in a mesh: tower: 8 (over z, x), plate: 4 (over y, core).
Axes of the slice: x: 2, y: 2, z: 4, core: 2. Of those that a mesh axis runs over, the one named last changes fastest.
Arguments:
- features: bfloat16 [8, 1024, 128], P('tower', 'plate'), may hold values from -6 to 6
- adjoint: bfloat16 [8, 1024, 128], P('tower', 'plate'), may hold values from -6 to 6
- positions: bfloat16 [3, 8, 1024], P(None, 'tower', 'plate'), may hold values from 0 to 1
- w_rbf: bfloat16 [16, 128], replicated, may hold values from -1.5 to 1.5
- b_rbf: float32 [128], replicated, may hold values from -1 to 1
- w_filter: bfloat16 [128, 128], replicated, may hold values from -0.5 to 0.5
- b_filter: float32 [128], replicated, may hold values from -1 to 1
- atom_counts: int32 [8, 4], P('tower', 'plate'), may hold values from 128 to 256, as said below
- tile_counts: int32 [8, 4], P('tower', 'plate'), may hold values from 1 to 56, as said below
- tower_tiles: int32 [8, 4, 56], P('tower', 'plate'), may hold values from 0 to 23
- plate_tiles: int32 [8, 4, 56], P('tower', 'plate'), may hold values from 0 to 31
- image_shifts: int32 [8, 4, 56], P('tower', 'plate'), may hold values from 0 to 8
Outputs:
- grad_features: float32 [8, 1024, 128], P('tower', 'plate')
- grad_positions: float32 [3, 8, 1024], P(None, 'tower', 'plate')
- grad_w_rbf: float32 [16, 128], replicated
- grad_b_rbf: float32 [128], replicated
- grad_w_filter: float32 [128, 128], replicated
- grad_b_filter: float32 [128], replicated
The draws below stay inside these ranges and needn't reach their ends.
Inputs may be any that keep to these rules, and one draw needn't show every extreme that they name: `atom_counts`: 256 in at least one brick. `tile_counts`: 56 in at least one brick; entries past the count are unused. `tower_tiles`: tiles below 8 lie in the brick below, the next 8 in the brick itself, the rest in the brick above. `plate_tiles`: tile v lies in brick v // 8 of the same plate. `image_shifts`: shift c moves the receiver by c // 3 - 1 along x and c % 3 - 1 along y.
All inputs are finite; a program needn't handle non-finite values.
Results may differ from the reference program's by a relative error of at most 0.005.
Values may be sent and summed in bfloat16 or wider, within the bound.
No kernel may reach another device: no remote copies, remote signals or barrier semaphores. Data moves between devices by JAX's collectives and lax.ppermute only.
A program may use at most 64 MiB of HBM per device.

```python
import math
import jax
import jax.numpy as jnp
from jax import lax

F = 128
NRBF = 16
ATOMS = 256
TILE = 32
MAXT = 56
TOWER_TILES = 24
BRICKS_Z = 8
BRICKS_XY = 4
PLATE_TILES = 32


def draw_atom_counts(key, part):
    key_one, key_two = jax.random.split(jax.random.fold_in(key, 11))
    bricks = BRICKS_Z * BRICKS_XY
    counts = jax.random.randint(key_one, (bricks,), ATOMS // 2, ATOMS + 1)
    chosen = jax.random.randint(key_two, (), 0, bricks)
    counts = jnp.where(jnp.arange(bricks) == chosen, ATOMS, counts)
    return counts.reshape(BRICKS_Z, BRICKS_XY).astype(jnp.int32)


def draw_tile_counts(key, part):
    key_one, key_two = jax.random.split(jax.random.fold_in(key, 23))
    bricks = BRICKS_Z * BRICKS_XY
    divisor = jax.random.randint(key_one, (bricks,), 1, 5)
    counts = jnp.maximum(1, MAXT // divisor)
    chosen = jax.random.randint(key_two, (), 0, bricks)
    counts = jnp.where(jnp.arange(bricks) == chosen, MAXT, counts)
    return counts.reshape(BRICKS_Z, BRICKS_XY).astype(jnp.int32)


def place_ends(drawn, own_key, smallest, largest):
    extent = drawn.shape
    index_at = [jax.random.randint(jax.random.fold_in(own_key, axis), (), 0, extent[axis]) for axis in range(len(extent))]
    drawn = drawn.at[tuple(index_at)].set(smallest)
    longest = extent.index(max(extent))
    index_at[longest] = (index_at[longest] + 1) % extent[longest]
    return drawn.at[tuple(index_at)].set(largest)


def steps_of(key, extent, shards, least, top_value):
    def one(position, parts):
        heights = jax.random.uniform(jax.random.fold_in(jax.random.fold_in(key, 6), position), (parts,), jnp.float32, least / len(shards), top_value / len(shards))
        return jnp.repeat(jnp.exp(heights), extent[position] // parts).reshape((-1,) + (1,) * (len(extent) - position - 1))

    loudness = one(*shards[0])
    for cut in shards[1:]:
        loudness = loudness * one(*cut)
    return loudness


def centred(key, shape, width, bound, shards=(), kind=jnp.bfloat16):
    entries = jax.random.normal(key, shape, jnp.float32) * width
    if len(shards) > 0:
        entries = steps_of(key, shape, shards, -0.22, 0.18) * entries
    return jnp.clip(entries, min=-bound, max=bound).astype(kind)


def setup_inputs(seed: int = 0) -> dict:
    keys = jax.random.split(jax.random.key(seed), 13)
    return {
        "features": centred(keys[0], (BRICKS_Z, BRICKS_XY * ATOMS, F), 1.0, 6.0, ((0, 8), (1, 4))),
        "adjoint": centred(keys[1], (BRICKS_Z, BRICKS_XY * ATOMS, F), 1.0, 6.0, ((0, 8), (1, 4))),
        "positions": jnp.clip(1.0 * jax.random.uniform(keys[2], (3, BRICKS_Z, BRICKS_XY * ATOMS), jnp.float32) ** steps_of(keys[2], (3, BRICKS_Z, BRICKS_XY * ATOMS), ((1, 8), (2, 4)), -0.2, 0.2), 0.0, 1.0).astype(jnp.bfloat16),
        "w_rbf": centred(keys[3], (NRBF, F), NRBF ** -0.5, 1.5),
        "b_rbf": jnp.clip(jax.random.uniform(keys[4], (F,), jnp.float32, -1.0, 1.0), -1.0, 1.0),
        "w_filter": centred(keys[5], (F, F), F ** -0.5, 0.5),
        "b_filter": jnp.clip(jax.random.uniform(keys[6], (F,), jnp.float32, -1.0, 1.0), -1.0, 1.0),
        "atom_counts": draw_atom_counts(jax.random.fold_in(keys[12], 71), 0),
        "tile_counts": draw_tile_counts(jax.random.fold_in(keys[12], 71), 0),
        "tower_tiles": place_ends(jax.random.randint(keys[9], (BRICKS_Z, BRICKS_XY, MAXT), 0, TOWER_TILES), jax.random.fold_in(keys[9], 1), 0, TOWER_TILES - 1).astype(jnp.int32),
        "plate_tiles": place_ends(jax.random.randint(keys[10], (BRICKS_Z, BRICKS_XY, MAXT), 0, PLATE_TILES), jax.random.fold_in(keys[10], 1), 0, PLATE_TILES - 1).astype(jnp.int32),
        "image_shifts": place_ends(jax.random.randint(keys[11], (BRICKS_Z, BRICKS_XY, MAXT), 0, 9), jax.random.fold_in(keys[11], 1), 0, 8).astype(jnp.int32),
    }


box_side = 1.0
brick_height = 1.0
cutoff_radius = 3.0
soften = 0.01
sharpness = 10.0
log_two = math.log(2.0)

def shift_vector(shift_code, tower_tile, per_brick):
    step_z = tower_tile // per_brick - 1
    return jnp.stack([(shift_code // 3 - 1).astype(jnp.float32) * box_side, (shift_code % 3 - 1).astype(jnp.float32) * box_side, step_z.astype(jnp.float32) * brick_height])

def pair_tile(adj_rows, recv_pos, feat_rows, send_pos, shift_vec, w_rbf, b_rbf, w_filter, b_filter):
    size_recv = adj_rows.shape[0]
    size_send = feat_rows.shape[0]
    feat_width = adj_rows.shape[1]
    displace = recv_pos[:, :, None] + shift_vec[:, None, None] - send_pos[:, None, :]
    distance = jnp.sqrt(lax.optimization_barrier(jnp.sum(displace * displace, axis=0)) + soften).reshape(-1)
    nbasis = w_rbf.shape[0]
    centres = jnp.arange(nbasis, dtype=jnp.float32) * (cutoff_radius / (nbasis - 1))
    offsets = distance[None, :] - centres[:, None]
    basis = jnp.exp(-sharpness * offsets * offsets)
    basis_b = basis.astype(jnp.bfloat16)
    preact = lax.dot_general(basis_b, w_rbf, (((0,), (0,)), ((), ())), preferred_element_type=jnp.float32) + b_rbf
    softed = (jax.nn.softplus(preact) - log_two).astype(jnp.bfloat16)
    filter_raw = jnp.dot(softed, w_filter, preferred_element_type=jnp.float32) + b_filter
    inside = distance < cutoff_radius
    phase_arg = math.pi / cutoff_radius * distance
    envelope = jnp.where(inside, 0.5 * (jnp.cos(phase_arg) + 1.0), 0.0)
    slope = jnp.where(inside, -0.5 * (math.pi / cutoff_radius) * jnp.sin(phase_arg), 0.0)
    adj_wide = adj_rows.astype(jnp.float32)
    feat_wide = feat_rows.astype(jnp.float32)
    filtered = (filter_raw * envelope[:, None]).reshape(size_recv, size_send, feat_width)
    grad_rows = jnp.einsum('if,ijf->jf', adj_wide, filtered)
    adjoint_pair = (adj_wide[:, None, :] * feat_wide[None, :, :]).reshape(size_recv * size_send, feat_width)
    d_raw = adjoint_pair * envelope[:, None]
    d_raw_b = d_raw.astype(jnp.bfloat16)
    grad_bf = lax.optimization_barrier(jnp.sum(d_raw, axis=0))
    grad_wf = lax.dot_general(softed, d_raw_b, (((0,), (0,)), ((), ())), preferred_element_type=jnp.float32)
    d_soft = lax.dot_general(d_raw_b, w_filter, (((1,), (1,)), ((), ())), preferred_element_type=jnp.float32)
    d_pre = d_soft * jax.nn.sigmoid(preact)
    d_pre_b = d_pre.astype(jnp.bfloat16)
    grad_br = lax.optimization_barrier(jnp.sum(d_pre, axis=0))
    grad_wr = lax.dot_general(basis_b, d_pre_b, (((1,), (0,)), ((), ())), preferred_element_type=jnp.float32)
    d_basis = lax.dot_general(w_rbf, d_pre_b, (((1,), (1,)), ((), ())), preferred_element_type=jnp.float32)
    d_dist = lax.optimization_barrier(jnp.sum(d_basis * basis * (-2.0 * sharpness) * offsets, axis=0))
    d_dist = d_dist + lax.optimization_barrier(jnp.sum(adjoint_pair * filter_raw, axis=1)) * slope
    radial = (d_dist / distance).reshape(size_recv, size_send)
    pull = displace * radial[None]
    return (grad_rows, lax.optimization_barrier(jnp.sum(pull, axis=2)), -lax.optimization_barrier(jnp.sum(pull, axis=1)), (grad_wr, grad_br, grad_wf, grad_bf))

def add_into(array, piece, starts):
    current = lax.dynamic_slice(array, starts, piece.shape)
    return lax.dynamic_update_slice(array, current + piece, starts)

def reference(features, adjoint, positions, w_rbf, b_rbf, w_filter, b_filter, atom_counts, tile_counts, tower_tiles, plate_tiles, image_shifts):
    tower_count = BRICKS_Z
    plate_count = BRICKS_XY
    per_brick = ATOMS // TILE
    feat_width = features.shape[2]
    slots = jnp.arange(ATOMS, dtype=jnp.int32)
    live_mask = (slots[None, None, :] < atom_counts[:, :, None]).reshape(tower_count, plate_count * ATOMS)
    zero_b = jnp.zeros((), jnp.bfloat16)
    feat_live = jnp.where(live_mask[:, :, None], features, zero_b)
    adj_live = jnp.where(live_mask[:, :, None], adjoint, zero_b)
    coords = positions.astype(jnp.float32)
    initial = (jnp.zeros(features.shape, jnp.float32), jnp.zeros(coords.shape, jnp.float32), (jnp.zeros(w_rbf.shape, jnp.float32), jnp.zeros(b_rbf.shape, jnp.float32), jnp.zeros(w_filter.shape, jnp.float32), jnp.zeros(b_filter.shape, jnp.float32)))

    def visit(index, totals):
        brick = index // MAXT
        entry = index % MAXT
        tower_i = (brick // plate_count).astype(jnp.int32)
        plate_i = (brick % plate_count).astype(jnp.int32)

        def work(totals):
            acc_dh, acc_gp, acc_weights = totals
            tower_tile = tower_tiles[tower_i, plate_i, entry]
            plate_tile = plate_tiles[tower_i, plate_i, entry]
            shift_code = image_shifts[tower_i, plate_i, entry]
            source_z = ((tower_i + tower_tile // per_brick - 1) % tower_count).astype(jnp.int32)
            recv_start = (plate_i * ATOMS + tower_tile % per_brick * TILE).astype(jnp.int32)
            send_start = (plate_tile * TILE).astype(jnp.int32)
            adj_rows = lax.dynamic_slice(adj_live, (source_z, recv_start, jnp.int32(0)), (1, TILE, feat_width))[0]
            recv_pos = lax.dynamic_slice(coords, (jnp.int32(0), source_z, recv_start), (3, 1, TILE))[:, 0]
            feat_rows = lax.dynamic_slice(feat_live, (tower_i, send_start, jnp.int32(0)), (1, TILE, feat_width))[0]
            send_pos = lax.dynamic_slice(coords, (jnp.int32(0), tower_i, send_start), (3, 1, TILE))[:, 0]
            shift_vec = shift_vector(shift_code, tower_tile, per_brick)
            grad_rows, grad_recv, grad_send, grad_weights = pair_tile(adj_rows, recv_pos, feat_rows, send_pos, shift_vec, w_rbf, b_rbf, w_filter, b_filter)
            acc_dh = add_into(acc_dh, grad_rows[None], (tower_i, send_start, jnp.int32(0)))
            acc_gp = add_into(acc_gp, grad_send[:, None, :], (jnp.int32(0), tower_i, send_start))
            acc_gp = add_into(acc_gp, grad_recv[:, None, :], (jnp.int32(0), source_z, recv_start))
            acc_weights = jax.tree.map(lambda left, right: left + right, acc_weights, grad_weights)
            return (acc_dh, acc_gp, acc_weights)
        return lax.cond(entry < tile_counts[tower_i, plate_i], work, lambda kept: kept, totals)
    acc_dh, acc_gp, acc_weights = lax.fori_loop(0, tower_count * plate_count * MAXT, visit, initial)
    total_tiles = jnp.sum(tile_counts).astype(jnp.float32)
    scale = 1.0 / jnp.sqrt(total_tiles * (TILE * TILE))
    grad_features = jnp.where(live_mask[:, :, None], acc_dh, 0.0)
    return (grad_features, acc_gp, acc_weights[0] * scale, acc_weights[1] * scale, acc_weights[2] * scale, acc_weights[3] * scale)
```

```python
import functools
import math

import jax
import jax.numpy as jnp
from jax import lax
from jax.experimental import pallas as pl
from jax.experimental.pallas import tpu as pltpu
from jax.sharding import PartitionSpec as P

TILE = 32
LANES = 128

box_side = 1.0
brick_height = 1.0
cutoff_radius = 3.0
soften = 0.01
sharpness = 10.0

F32 = jnp.float32
BF16 = jnp.bfloat16


def up(value, unit):
    return -(-value // unit) * unit


def iota(shape, axis):
    return lax.broadcasted_iota(jnp.int32, shape, axis)


def one_hot(cond):
    return jnp.where(cond, 1.0, 0.0).astype(BF16)


def nn(left, right):
    return lax.dot_general(left, right, (((1,), (0,)), ((), ())), preferred_element_type=F32)


def nt(left, right):
    return lax.dot_general(left, right, (((1,), (1,)), ((), ())), preferred_element_type=F32)


def split(value, parts):
    pieces = []
    for _ in range(parts):
        piece = value.astype(BF16)
        pieces.append(piece)
        value = value - piece.astype(F32)
    return pieces


def nn_split(left, right):
    pieces = split(left, 2)
    return nn(pieces[0], right) + nn(pieces[1], right)


def poly(square, coefs):
    total = jnp.full_like(square, coefs[-1])
    for coef in coefs[-2::-1]:
        total = total * square + coef
    return total


SIN = [(-1.0) ** n / math.factorial(2 * n + 1) for n in range(7)]
COS = [(-1.0) ** n / math.factorial(2 * n) for n in range(8)]


def pack_kernel(count_ref, feat_ref, adj_ref, pos_ref, out_feat, out_adj):
    atoms, width = feat_ref.shape[1:]
    live = iota((atoms, width), 0) < count_ref[0, 0]
    rows = atoms // LANES
    extra = out_feat.shape[0] - atoms
    parts = [
        pos_ref[axis, :, r * LANES : (r + 1) * LANES] for axis in range(3) for r in range(rows)
    ]
    parts.append(jnp.zeros((extra - len(parts), width), BF16))
    tail = jnp.concatenate([part.astype(F32) for part in parts], axis=0).astype(BF16)
    for source, target in ((feat_ref, out_feat), (adj_ref, out_adj)):
        kept = jnp.where(live, source[0].astype(F32), 0.0)
        target[:atoms] = kept.astype(BF16)
        target[atoms:] = tail


def tile_kernel(
    plate_count,
    where_ref,
    count_ref,
    tower_ref,
    plate_ref,
    shift_ref,
    *refs,
):
    (own_adj, near_adj, far_adj), refs = refs[:3], refs[3:]
    feats, refs = refs[:plate_count], refs[plate_count:]
    (w_rbf_ref, b_rbf_ref, w_filter_ref, b_filter_ref), refs = refs[:4], refs[4:]
    (keep_out, send_out, weight_out, near_out, far_out), refs = refs[:5], refs[5:]
    (
        adj_wide,
        adj_full,
        feat_wide,
        recv_wide,
        send_wide,
        grad_feat,
        grad_recv,
        grad_send,
        acc_wf,
        acc_wr,
        lhs_x,
        lhs_f,
        lhs_a,
        lhs_d,
    ), refs = refs[:14], refs[14:]
    slots = (refs[: len(refs) // 2], refs[len(refs) // 2 :])
    width = w_filter_ref.shape[0]
    nbasis = w_rbf_ref.shape[0]
    block_rows = own_adj.shape[0]
    groups = LANES // TILE
    chunks = TILE // groups
    pairs = TILE * TILE
    per_brick = adj_wide.shape[0] // 3
    atoms = per_brick * TILE
    rows = atoms // LANES
    spots = 3 * rows
    tower_at = where_ref[0]
    plate_at = where_ref[1]
    odd = lax.rem(tower_at, 2)
    near_slot = 2 - 2 * odd
    far_slot = 2 * odd
    sources = ((far_adj, far_slot), (own_adj, 1), (near_adj, near_slot))

    pick_recv = one_hot(iota((TILE, pairs), 0) == iota((TILE, pairs), 1) // TILE)
    pick_send = one_hot(iota((TILE, LANES), 0) == iota((TILE, LANES), 1) % TILE)
    for source, slot in sources:

        def widen_adj(half, carry, source=source, slot=slot):
            for t in (2 * half, 2 * half + 1):
                start = pl.multiple_of(t * TILE, TILE)
                part = source[pl.ds(start, TILE), :].astype(F32).T.astype(BF16)
                wide = nn(part, pick_recv)
                adj_full[slot * per_brick + t] = wide
                adj_wide[slot * per_brick + t] = wide.astype(BF16)
            return carry

        lax.fori_loop(0, per_brick // 2, widen_adj, 0)
    for q in range(groups):
        pick = one_hot(iota((LANES, pairs), 0) == q * TILE + iota((LANES, pairs), 1) // TILE)
        for source, slot in sources:
            wide = nn(source[atoms:block_rows], pick)
            for c in range(chunks):
                recv_wide[slot, q, :, c, :] = wide[:spots, c * LANES : (c + 1) * LANES]
    for q in range(groups):
        pick = one_hot(iota((LANES, LANES), 0) == q * TILE + iota((LANES, LANES), 1) % TILE)
        for step, source in enumerate(feats):
            send_wide[plate_at ^ step, q] = nn(source[atoms:block_rows], pick)
    for step, source in enumerate(feats):
        brick = plate_at ^ step

        def widen_feat(half, carry, source=source, brick=brick):
            for t in range(4):
                t = 4 * half + t
                start = pl.multiple_of(t * TILE, TILE)
                part = source[pl.ds(start, TILE), :].astype(F32).T.astype(BF16)
                feat_wide[brick * per_brick + t] = nn(part, pick_send).astype(BF16)
            return carry

        lax.fori_loop(0, per_brick // 4, widen_feat, 0)

    w_rbf = w_rbf_ref[...].astype(F32)
    half_bias = [piece.astype(F32) for piece in split(0.5 * b_rbf_ref[...], 3)]
    stacked = jnp.concatenate(
        [0.5 * w_rbf] + half_bias + [jnp.zeros((LANES - nbasis - 3, width), F32)], axis=0
    )
    lhs_x[...] = stacked.T[:, : 2 * nbasis].astype(BF16)
    w_filter = w_filter_ref[...].astype(F32)
    bias = [piece.astype(F32) for piece in split(b_filter_ref[...], 3)]
    bias = jnp.concatenate(bias + [jnp.zeros((LANES - 3, width), F32)], axis=0)
    lhs_f[:, :width] = w_filter.T.astype(BF16)
    lhs_f[:, width:] = bias.T.astype(BF16)
    lhs_a[:width] = w_filter_ref[...]
    lhs_a[width:] = bias[:16].astype(BF16)
    lhs_d[:nbasis, :width] = w_rbf_ref[...]
    lhs_d[nbasis:, :width] = jnp.zeros((nbasis, width), BF16)
    lhs_d[:nbasis, width:] = jnp.zeros((nbasis, width), BF16)
    lhs_d[nbasis:, width:] = one_hot(iota((nbasis, width), 0) == 0)

    grad_feat[...] = jnp.zeros_like(grad_feat)
    grad_recv[...] = jnp.zeros_like(grad_recv)
    grad_send[...] = jnp.zeros_like(grad_send)
    acc_wf[...] = jnp.zeros_like(acc_wf)
    acc_wr[...] = jnp.zeros_like(acc_wr)

    count = count_ref[0, 0]
    span = 2 * LANES
    centres = iota((nbasis, span), 0).astype(F32) * (cutoff_radius / (nbasis - 1))
    ones_rows = jnp.ones((nbasis, span), BF16)

    def places(entry):
        entry = jnp.minimum(entry, count - 1)
        tower_tile = tower_ref[0, 0, entry]
        plate_tile = plate_ref[0, 0, entry]
        recv_t = tower_tile % per_brick
        send_t = plate_tile % per_brick
        recv = (tower_tile // per_brick, recv_t % groups, recv_t // groups)
        send = (plate_tile // per_brick, send_t % groups, send_t // groups)
        return tower_tile, plate_tile, recv, send, shift_ref[0, 0, entry]

    def start_tile(entry, slot):
        stack_ref, soft_ref, gate_ref, basis_ref, slant_ref, geo_ref, _ = slot
        _, _, recv_at, send_at, code = places(entry)
        shifts = (
            (code // 3 - 1).astype(F32) * box_side,
            (code % 3 - 1).astype(F32) * box_side,
            (recv_at[0] - 1).astype(F32) * brick_height,
        )
        square = soften
        for axis in range(3):
            recv = recv_wide[recv_at[0], recv_at[1], axis * rows + recv_at[2]]
            send = send_wide[send_at[0], send_at[1], pl.ds(axis * rows + send_at[2], 1), :]
            disp = recv + shifts[axis] - send
            geo_ref[axis] = disp
            square = square + disp * disp
        dist = jnp.sqrt(square)
        reach = jnp.where(entry < count, cutoff_radius, 0.0)
        inside = dist < reach
        angle = (0.5 * math.pi / cutoff_radius) * (cutoff_radius - dist)
        square = angle * angle
        sine = angle * poly(square, SIN)
        cosine = poly(square, COS)
        envelope = jnp.where(inside, sine * sine, 0.0)
        geo_ref[3] = jnp.where(inside, (-math.pi / cutoff_radius) * sine * cosine, 0.0)
        geo_ref[4] = 1.0 / dist

        def chunk(c):
            def row(value):
                return jnp.concatenate([value[c : c + 1], value[c + 1 : c + 2]], axis=1)

            at = slice(c * LANES, c * LANES + span)
            offsets = row(dist) - centres
            basis = jnp.exp(-sharpness * offsets * offsets)
            basis_b = jnp.concatenate([basis.astype(BF16), ones_rows], axis=0)
            basis_ref[:, at] = basis_b
            slant_ref[:, at] = (-2.0 * sharpness) * basis * offsets
            tanh = jnp.tanh(nn(lhs_x[...], basis_b))
            neg_soft = jnp.log(1.0 - tanh).astype(BF16)
            env = row(envelope)
            env16 = jnp.broadcast_to(env, (16, span))
            soft_ref[:, at] = neg_soft
            gate_ref[:, at] = (tanh + 1.0) * (0.5 * env)
            stack_ref[:width, at] = (
                neg_soft.reshape(-1, 16, span) * (-env16).astype(BF16)[None]
            ).reshape(width, span)
            stack_ref[width:, at] = env16.astype(BF16)

        return chunk

    def finish_tile(entry, slot):
        stack_ref, soft_ref, gate_ref, basis_ref, slant_ref, geo_ref, pull_ref = slot
        tower_tile, plate_tile, recv_at, send_at, _ = places(entry)
        sums = []

        def chunk(c):
            at = slice(c * LANES, c * LANES + span)
            feat = feat_wide[plate_tile]
            pair = adj_wide[tower_tile, :, at] * jnp.concatenate([feat, feat], axis=1)
            stack = stack_ref[:, at]
            filt = nn(lhs_f[:, : width + 16], stack)
            back = nn(lhs_a[...], pair)
            part_wf = nt(stack, pair)
            prod = filt * adj_full[tower_tile, :, at]
            prod = prod[:, :LANES] + prod[:, LANES:]
            d_pre = (back[:width] * gate_ref[:, at]).astype(BF16)
            both = jnp.concatenate([d_pre, soft_ref[:, at] * back[:width].astype(BF16)], axis=0)
            part_wr = nt(basis_ref[:, at], d_pre)
            d_basis = nn(lhs_d[...], both)
            direct = jnp.sum(d_basis[:nbasis] * slant_ref[:, at], axis=0, keepdims=True)
            inner = jnp.sum(back[width : width + 8], axis=0, keepdims=True)
            inner = inner - d_basis[nbasis : nbasis + 1]
            pull_ref[c : c + 1, :] = direct[:, :LANES] + geo_ref[3, c : c + 1] * inner[:, :LANES]
            pull_ref[c + 1 : c + 2, :] = (
                direct[:, LANES:] + geo_ref[3, c + 1 : c + 2] * inner[:, LANES:]
            )
            parts = [prod, part_wf, part_wr]
            sums[:] = [a + b for a, b in zip(sums, parts)] if sums else parts

        def end():
            radial = pull_ref[...] * geo_ref[4]
            for axis in range(3):
                pull = geo_ref[axis] * radial
                grad_recv[recv_at[0], recv_at[1], axis * rows + recv_at[2]] += pull
                grad_send[send_at[0], send_at[1], axis * rows + send_at[2]] += pull
            grad_feat[plate_tile] += sums[0]
            acc_wf[...] += sums[1]
            acc_wr[...] += sums[2]

        return chunk, end

    first = start_tile(0, slots[0])
    for c in range(0, chunks, 2):
        first(c)

    def visit(step, carry):
        for n in range(2):
            entry = 2 * step + n
            ahead = start_tile(entry + 1, slots[1 - n])
            chunk, end = finish_tile(entry, slots[n])
            for c in range(0, chunks, 2):
                ahead(c)
                chunk(c)
            end()
        return carry

    lax.fori_loop(0, (count + 1) // 2, visit, 0)

    digit = iota((1, width), 1)
    count_row = jnp.where(digit == 0, lax.rem(count, 16), 0)
    count_row = jnp.where(digit == 1, count // 16, count_row).astype(F32)
    weights = jnp.concatenate(
        [
            acc_wf[:width],
            acc_wr[:nbasis],
            acc_wf[width : width + 1],
            acc_wr[nbasis : nbasis + 1],
            count_row,
            jnp.zeros((weight_out.shape[0] - width - nbasis - 3, width), F32),
        ],
        axis=0,
    )
    weight_out[...] = weights
    put_split(send_out, weights)

    fold = one_hot(iota((TILE, LANES), 0) == iota((TILE, LANES), 1) % TILE)
    same_slot = one_hot(iota((LANES, LANES), 0) % TILE == iota((LANES, LANES), 1) % TILE)
    same_group = one_hot(iota((LANES, LANES), 0) // TILE == iota((LANES, LANES), 1) % groups)
    group_of = iota((spots, LANES), 1) // TILE
    padding = jnp.zeros((block_rows - atoms - spots, LANES), F32)
    for step in range(plate_count):
        brick = plate_at ^ step
        at = step // 2 * block_rows
        target = send_out if step % 2 else keep_out
        kind = target.dtype

        def fold_feat(half, carry, brick=brick, at=at, target=target, kind=kind):
            for t in range(4):
                t = 4 * half + t
                pieces = split(grad_feat[brick * per_brick + t], 2)
                start = pl.multiple_of(at + t * TILE, 16)
                target[pl.ds(start, TILE), :] = (
                    nt(fold, pieces[0]) + nt(fold, pieces[1])
                ).astype(kind)
            return carry

        lax.fori_loop(0, per_brick // 4, fold_feat, 0)
        total = jnp.zeros((spots, LANES), F32)
        for q in range(groups):
            summed = nn_split(jnp.sum(grad_send[brick, q], axis=1), same_slot)
            total = jnp.where(group_of == q, -summed, total)
        total = jnp.concatenate([total, padding], axis=0)
        target[at + atoms : at + block_rows] = total.astype(kind)
    lane = iota((chunks, LANES), 1)
    own_chunk = (lane // groups) % chunks == iota((chunks, LANES), 0)
    for target, slot in ((far_out, far_slot), (None, 1), (near_out, near_slot)):
        total = jnp.zeros((spots, chunks, LANES), F32)
        for q in range(groups):
            summed = nn_split(grad_recv[slot, q].reshape(spots * chunks, LANES), same_group)
            chosen = own_chunk & (lane // TILE == q)
            total = total + jnp.where(chosen[None], summed.reshape(spots, chunks, LANES), 0.0)
        total = jnp.concatenate([jnp.sum(total, axis=1), padding], axis=0)
        if target is None:
            keep_out[atoms:block_rows] += total
        else:
            target[...] = total


def put_split(target, weights):
    count = weights.shape[0]
    end = target.shape[0]
    high, low = split(weights, 2)
    target[end - 2 * count : end - count] = high
    target[end - count :] = low


def add_kernel(cut, kept_ref, weight_ref, got_ref, kept_out, *outs):
    held, count = kept_ref.shape[0], weight_ref.shape[0]
    got = got_ref[...].astype(F32)
    total = kept_ref[...] + got[:held]
    weights = weight_ref[...] + got[held : held + count] + got[held + count :]
    kept_out[...] = total[:cut]
    outs[-1][...] = weights
    if len(outs) == 2:
        outs[0][: held - cut] = total[cut:].astype(BF16)
        put_split(outs[0], weights)


def finish_kernel(atoms, count_ref, block_ref, near_ref, far_ref, feat_out, pos_out):
    width = block_ref.shape[1]
    live = iota((atoms, width), 0) < count_ref[0, 0]
    feat_out[0] = jnp.where(live, block_ref[:atoms], 0.0)
    spots = block_ref[atoms:] + near_ref[...] + far_ref[...]
    rows = atoms // LANES
    for axis in range(3):
        for r in range(rows):
            at = axis * rows + r
            pos_out[axis, :, r * LANES : (r + 1) * LANES] = spots[at : at + 1]


def weight_kernel(*refs):
    ins, outs = refs[:-4], refs[-4:]
    total = ins[0][...]
    for other in ins[1:]:
        total = total + other[...]
    nbasis, width = outs[0].shape
    row = total[width + nbasis + 2 : width + nbasis + 3]
    tiles = row[:, :1] + 16.0 * row[:, 1:2]
    scale = lax.rsqrt(tiles * (TILE * TILE))
    outs[0][...] = total[width : width + nbasis] * scale
    outs[1][...] = total[width + nbasis + 1 : width + nbasis + 2] * scale
    outs[2][...] = total[:width] * scale
    outs[3][...] = total[width + nbasis : width + nbasis + 1] * scale


def swap(value, axis, route):
    size = lax.axis_size(axis)
    return lax.ppermute(value, axis, [(i, route(i) % size) for i in range(size)])


def across(bits):
    return lambda i: i ^ bits


def beyond(i):
    return i + 1 if i % 2 else i - 1


VMEM = pl.BlockSpec(memory_space=pltpu.VMEM)
SMEM = pl.BlockSpec(memory_space=pltpu.SMEM)


def call(kernel, name, shapes, places, **extra):
    return pl.pallas_call(
        kernel,
        name=name,
        out_shape=[jax.ShapeDtypeStruct(shape, kind) for shape, kind in shapes],
        in_specs=places,
        out_specs=[VMEM] * len(shapes),
        **extra,
    )


def local(
    features,
    adjoint,
    positions,
    w_rbf,
    b_rbf,
    w_filter,
    b_filter,
    atom_counts,
    tile_counts,
    tower_tiles,
    plate_tiles,
    image_shifts,
):
    atoms, width = features.shape[1:]
    nbasis = w_rbf.shape[0]
    per_brick = atoms // TILE
    groups = LANES // TILE
    chunks = TILE // groups
    plate_count = lax.axis_size("plate")
    tower_count = lax.axis_size("tower")
    if plate_count & (plate_count - 1) or tower_count & (tower_count - 1):
        raise ValueError("axis sizes")
    pairs = TILE * TILE
    spots = 3 * (atoms // LANES)
    spot_rows = up(spots, 16)
    block = atoms + spot_rows
    weight_rows = up(width + nbasis + 3, 16)

    feat_block, adj_block = call(
        pack_kernel,
        "pack",
        [((block, width), BF16)] * 2,
        [SMEM, VMEM, VMEM, VMEM],
    )(atom_counts, features, adjoint, positions)
    peers = [swap(feat_block, "plate", across(step)) for step in range(1, plate_count)]
    near_adj = swap(adj_block, "tower", across(1))
    far_adj = swap(adj_block, "tower", beyond)

    at = jnp.stack([lax.axis_index("tower"), lax.axis_index("plate")]).astype(jnp.int32)
    half = plate_count // 2
    keep, send, weights, near_pos, far_pos = call(
        functools.partial(tile_kernel, plate_count),
        "tiles",
        [
            ((half * block, width), F32),
            ((half * block + 2 * weight_rows, width), BF16),
            ((weight_rows, width), F32),
            ((spot_rows, width), F32),
            ((spot_rows, width), F32),
        ],
        [SMEM] * 5 + [VMEM] * (3 + plate_count + 4),
        scratch_shapes=[
            pltpu.VMEM((3 * per_brick, width, pairs), BF16),
            pltpu.VMEM((3 * per_brick, width, pairs), F32),
            pltpu.VMEM((plate_count * per_brick, width, LANES), BF16),
            pltpu.VMEM((3, groups, spots, chunks, LANES), F32),
            pltpu.VMEM((plate_count, groups, spot_rows, LANES), F32),
            pltpu.VMEM((plate_count * per_brick, width, LANES), F32),
            pltpu.VMEM((3, groups, spots, chunks, LANES), F32),
            pltpu.VMEM((plate_count, groups, spots, chunks, LANES), F32),
            pltpu.VMEM((width + 16, width), F32),
            pltpu.VMEM((2 * nbasis, width), F32),
            pltpu.VMEM((width, 2 * nbasis), BF16),
            pltpu.VMEM((width, 2 * width), BF16),
            pltpu.VMEM((width + 16, width), BF16),
            pltpu.VMEM((2 * nbasis, 2 * width), BF16),
        ]
        + [
            pltpu.VMEM((width + 16, pairs), BF16),
            pltpu.VMEM((width, pairs), BF16),
            pltpu.VMEM((width, pairs), F32),
            pltpu.VMEM((2 * nbasis, pairs), BF16),
            pltpu.VMEM((nbasis, pairs), F32),
            pltpu.VMEM((5, chunks, LANES), F32),
            pltpu.VMEM((chunks, LANES), F32),
        ]
        * 2,
    )(
        at,
        tile_counts,
        tower_tiles,
        plate_tiles,
        image_shifts,
        adj_block,
        near_adj,
        far_adj,
        feat_block,
        *peers,
        w_rbf,
        b_rbf[None],
        w_filter,
        b_filter[None],
    )

    got_near, got_far = None, None
    for step in [1] + [1 << n for n in reversed(range(1, plate_count.bit_length() - 1))]:
        got = swap(send, "plate", across(step))
        if got_near is None:
            got_near = swap(near_pos, "tower", across(1))
            got_far = swap(far_pos, "tower", beyond)
        held = keep.shape[0]
        cut = max(held // 2, block)
        shapes = [((cut, width), F32)]
        if held > cut:
            shapes.append(((held - cut + 2 * weight_rows, width), BF16))
        shapes.append(((weight_rows, width), F32))
        keep, *rest = call(functools.partial(add_kernel, cut), "add", shapes, [VMEM] * 3)(
            keep, weights, got
        )
        weights = rest[-1]
        send = rest[0]
    grad_features, grad_positions = call(
        functools.partial(finish_kernel, atoms),
        "finish",
        [((1, atoms, width), F32), ((3, 1, atoms), F32)],
        [SMEM, VMEM, VMEM, VMEM],
    )(atom_counts, keep, got_near, got_far)

    weights = weights + swap(weights, "tower", across(1))
    bits = 2
    parts = [weights]
    while bits < tower_count:
        weights = sum(parts[1:], parts[0])
        stride = [s * bits for s in (1, 2, 3) if s * bits < tower_count]
        parts = [weights] + [swap(weights, "tower", across(s)) for s in stride]
        bits *= 4
    out_wr, out_br, out_wf, out_bf = call(
        weight_kernel,
        "weights",
        [((nbasis, width), F32), ((1, width), F32), ((width, width), F32), ((1, width), F32)],
        [VMEM] * len(parts),
    )(*parts)
    return grad_features, grad_positions, out_wr, out_br[0], out_wf, out_bf[0]


def solution(mesh):
    in_specs = (
        P("tower", "plate", None),
        P("tower", "plate", None),
        P(None, "tower", "plate"),
        P(),
        P(),
        P(),
        P(),
        P("tower", "plate"),
        P("tower", "plate"),
        P("tower", "plate", None),
        P("tower", "plate", None),
        P("tower", "plate", None),
    )
    out_specs = (P("tower", "plate", None), P(None, "tower", "plate"), P(), P(), P(), P())
    return jax.shard_map(local, mesh=mesh, in_specs=in_specs, out_specs=out_specs, check_vma=False)
```

```python
import functools
import math

import jax
import jax.numpy as jnp
from jax import lax
from jax.experimental import pallas as pl
from jax.experimental.pallas import tpu as pltpu
from jax.sharding import PartitionSpec as P


TILE = 32
LANES = 128
PART = 32

box_side = 1.0
brick_height = 1.0
cutoff_radius = 3.0
soften = 0.01
sharpness = 10.0

F32 = jnp.float32
BF16 = jnp.bfloat16


def up(value, unit):
    return -(-value // unit) * unit


def iota(shape, axis):
    return lax.broadcasted_iota(jnp.int32, shape, axis)


def one_hot(cond):
    return jnp.where(cond, 1.0, 0.0).astype(BF16)


def nn(left, right):
    return lax.dot_general(left, right, (((1,), (0,)), ((), ())), preferred_element_type=F32)


def nt(left, right):
    return lax.dot_general(left, right, (((1,), (1,)), ((), ())), preferred_element_type=F32)


def split(value, parts):
    pieces = []
    for _ in range(parts):
        piece = value.astype(BF16)
        pieces.append(piece)
        value = value - piece.astype(F32)
    return pieces


def nn_split(left, right):
    pieces = split(left, 2)
    return nn(pieces[0], right) + nn(pieces[1], right)


def poly(square, coefs):
    total = jnp.full_like(square, coefs[-1])
    for coef in coefs[-2::-1]:
        total = total * square + coef
    return total


SIN = [(-1.0) ** n / math.factorial(2 * n + 1) for n in range(7)]
COS = [(-1.0) ** n / math.factorial(2 * n) for n in range(8)]


def pack_kernel(count_ref, feat_ref, adj_ref, pos_ref, out_feat, out_adj):
    atoms, width = feat_ref.shape[1:]
    live = iota((atoms, width), 0) < count_ref[0, 0]
    rows = atoms // LANES
    extra = out_feat.shape[0] - atoms
    parts = [
        pos_ref[axis, :, r * LANES : (r + 1) * LANES] for axis in range(3) for r in range(rows)
    ]
    parts.append(jnp.zeros((extra - len(parts), width), F32))
    tail = jnp.concatenate(parts, axis=0).astype(BF16)
    for source, target in ((feat_ref, out_feat), (adj_ref, out_adj)):
        kept = jnp.where(live, source[0].astype(F32), 0.0)
        target[:atoms] = kept.astype(BF16)
        target[atoms:] = tail


def tile_kernel(
    plate_count,
    where_ref,
    count_ref,
    tower_ref,
    plate_ref,
    shift_ref,
    *refs,
):
    (own_adj, near_adj, far_adj), refs = refs[:3], refs[3:]
    feats, refs = refs[:plate_count], refs[plate_count:]
    (w_rbf_ref, b_rbf_ref, w_filter_ref, b_filter_ref), refs = refs[:4], refs[4:]
    (keep_out, send_out, weight_out, near_out, far_out), refs = refs[:5], refs[5:]
    (
        adj_wide,
        feat_wide,
        recv_wide,
        send_wide,
        grad_feat,
        grad_recv,
        grad_send,
        acc_wf,
        acc_wr,
        lhs_x,
        lhs_f,
        lhs_a,
        lhs_d,
    ), refs = refs[:13], refs[13:]
    stack_buf, soft_buf, gate_buf, pair_buf, both_buf, refs = *refs[:5], refs[5:]
    basis_buf, slant_buf, inner_buf, geo_buf, pull_buf, *refs = refs
    half_buf, back_buf, filt_buf = refs
    width = w_filter_ref.shape[0]
    nbasis = w_rbf_ref.shape[0]
    block_rows = own_adj.shape[0]
    groups = LANES // TILE
    chunks = TILE // groups
    pairs = TILE * TILE
    per_brick = adj_wide.shape[0] // 3
    atoms = per_brick * TILE
    rows = atoms // LANES
    spots = 3 * rows
    tower_at = where_ref[0]
    plate_at = where_ref[1]
    odd = lax.rem(tower_at, 2)
    near_slot = 2 - 2 * odd
    far_slot = 2 * odd
    sources = ((far_adj, far_slot), (own_adj, 1), (near_adj, near_slot))

    pick_recv = one_hot(iota((TILE, pairs), 0) == iota((TILE, pairs), 1) // TILE)
    pick_send = one_hot(iota((TILE, LANES), 0) == iota((TILE, LANES), 1) % TILE)
    for source, slot in sources:

        def widen_adj(half, carry, source=source, slot=slot):
            for t in (2 * half, 2 * half + 1):
                start = pl.multiple_of(t * TILE, TILE)
                part = source[pl.ds(start, TILE), :].astype(F32).T.astype(BF16)
                wide = nn(part, pick_recv)
                for c in range(chunks):
                    adj_wide[slot * per_brick + t, c] = wide[:, c * LANES : (c + 1) * LANES]
            return carry

        lax.fori_loop(0, per_brick // 2, widen_adj, 0)
    for q in range(groups):
        pick = one_hot(iota((LANES, pairs), 0) == q * TILE + iota((LANES, pairs), 1) // TILE)
        for source, slot in sources:
            wide = nn(source[atoms:block_rows], pick)
            for c in range(chunks):
                recv_wide[slot, q, :, c, :] = wide[:spots, c * LANES : (c + 1) * LANES]
    for q in range(groups):
        pick = one_hot(iota((LANES, LANES), 0) == q * TILE + iota((LANES, LANES), 1) % TILE)
        for step, source in enumerate(feats):
            send_wide[plate_at ^ step, q] = nn(source[atoms:block_rows], pick)
    for step, source in enumerate(feats):
        brick = plate_at ^ step

        def widen_feat(half, carry, source=source, brick=brick):
            for t in range(4):
                t = 4 * half + t
                start = pl.multiple_of(t * TILE, TILE)
                part = source[pl.ds(start, TILE), :].astype(F32).T.astype(BF16)
                feat_wide[brick * per_brick + t] = nn(part, pick_send)
            return carry

        lax.fori_loop(0, per_brick // 4, widen_feat, 0)

    w_rbf = w_rbf_ref[...].astype(F32)
    half_bias = [piece.astype(F32) for piece in split(0.5 * b_rbf_ref[...], 3)]
    stacked = jnp.concatenate(
        [0.5 * w_rbf] + half_bias + [jnp.zeros((LANES - nbasis - 3, width), F32)], axis=0
    )
    lhs_x[...] = stacked.T[:, : 2 * nbasis].astype(BF16)
    w_filter = w_filter_ref[...].astype(F32)
    bias = [piece.astype(F32) for piece in split(b_filter_ref[...], 3)]
    bias = jnp.concatenate(bias + [jnp.zeros((LANES - 3, width), F32)], axis=0)
    lhs_f[0] = w_filter.T.astype(BF16)
    lhs_f[1] = bias.T.astype(BF16)
    lhs_a[:width] = w_filter_ref[...]
    lhs_a[width:] = bias[:16].astype(BF16)
    lhs_d[0, :nbasis] = w_rbf_ref[...]
    lhs_d[0, nbasis:] = jnp.zeros((nbasis, width), BF16)
    lhs_d[1, :nbasis] = jnp.zeros((nbasis, width), BF16)
    lhs_d[1, nbasis:] = one_hot(iota((nbasis, width), 0) == 0)

    grad_feat[...] = jnp.zeros_like(grad_feat)
    grad_recv[...] = jnp.zeros_like(grad_recv)
    grad_send[...] = jnp.zeros_like(grad_send)
    acc_wf[...] = jnp.zeros_like(acc_wf)
    acc_wr[...] = jnp.zeros_like(acc_wr)

    count = count_ref[0, 0]
    span = 2 * LANES
    centres = iota((nbasis, LANES), 0).astype(F32) * (cutoff_radius / (nbasis - 1))
    ones_rows = jnp.ones((nbasis, LANES), BF16)

    def places(entry):
        entry = jnp.minimum(entry, count - 1)
        tower_tile = tower_ref[0, 0, entry]
        plate_tile = plate_ref[0, 0, entry]
        recv_t = tower_tile % per_brick
        send_t = plate_tile % per_brick
        recv = (tower_tile // per_brick, recv_t % groups, recv_t // groups)
        send = (plate_tile // per_brick, send_t % groups, send_t // groups)
        return tower_tile, plate_tile, recv, send, shift_ref[0, 0, entry]

    per_tile = pairs // span
    ring = 2 * per_tile

    def blocks_of(at):
        return (at % ring * 2, at % ring * 2 + 1)

    def wide(ref, blocks, rows=slice(None)):
        return jnp.concatenate([ref[n, rows] for n in blocks], axis=1)

    def geometry(entry, tile):
        _, _, recv_at, send_at, code = places(entry)
        shifts = (
            (code // 3 - 1).astype(F32) * box_side,
            (code % 3 - 1).astype(F32) * box_side,
            (recv_at[0] - 1).astype(F32) * brick_height,
        )
        square = soften
        for axis in range(3):
            recv = recv_wide[recv_at[0], recv_at[1], axis * rows + recv_at[2]]
            send = send_wide[send_at[0], send_at[1], pl.ds(axis * rows + send_at[2], 1), :]
            disp = recv + shifts[axis] - send
            geo_buf[tile, axis] = disp
            square = square + disp * disp
        dist = jnp.sqrt(square)
        inside = dist < jnp.where(entry < count, cutoff_radius, 0.0)
        angle = (0.5 * math.pi / cutoff_radius) * (cutoff_radius - dist)
        square = angle * angle
        sine = angle * poly(square, SIN)
        cosine = poly(square, COS)
        geo_buf[tile, 3] = jnp.where(inside, (-math.pi / cutoff_radius) * sine * cosine, 0.0)
        geo_buf[tile, 4] = 1.0 / dist
        geo_buf[tile, 5] = dist
        geo_buf[tile, 6] = jnp.where(inside, sine * sine, 0.0)

    def geo_row(at, which):
        tile, c = at // per_tile % 2, at % per_tile * 2
        return [geo_buf[tile, which, n : n + 1] for n in (c, c + 1)]

    def basis_stage(at):
        for n, dist in zip(blocks_of(at), geo_row(at, 5)):
            offsets = dist - centres
            basis = jnp.exp(-sharpness * offsets * offsets)
            slant_buf[n] = (-2.0 * sharpness) * basis * offsets
            basis_buf[n] = jnp.concatenate([basis.astype(BF16), ones_rows], axis=0)
        half = nn(lhs_x[...], wide(basis_buf, blocks_of(at)))
        half_buf[at % 2 * 2] = half[:, :LANES]
        half_buf[at % 2 * 2 + 1] = half[:, LANES:]

    def soft_stage(at, entry):
        tower_tile, plate_tile = places(entry)[:2]
        c = at % per_tile * 2
        for n, block in enumerate(blocks_of(at)):
            env_rows = jnp.broadcast_to(geo_row(at, 6)[n], (PART, LANES))
            half_env = 0.5 * env_rows
            log_env = -math.log(2.0) * env_rows
            stack_buf[block, width:] = env_rows[:16].astype(BF16)
            for r in parts:
                tanh = jnp.tanh(half_buf[at % 2 * 2 + n, r])
                soft = jnp.log2(1.0 - tanh)
                soft_buf[block, r] = soft
                stack_buf[block, r] = (soft * log_env).astype(BF16)
                gate_buf[block, r] = (tanh + 1.0) * half_env
                pair = adj_wide[tower_tile, c + n, r] * feat_wide[plate_tile, r]
                pair_buf[block, r] = pair.astype(BF16)

    def product_stage(at):
        blocks = blocks_of(at)
        back = nn(lhs_a[...], wide(pair_buf, blocks))
        lhs = jnp.concatenate([lhs_f[0], lhs_f[1, :, :16]], axis=1)
        filt = nn(lhs, wide(stack_buf, blocks))
        for n in range(2):
            back_buf[at % 2 * 2 + n] = back[:, n * LANES : (n + 1) * LANES]
            filt_buf[at % 2 * 2 + n] = filt[:, n * LANES : (n + 1) * LANES]

    def feature_stage(at, entry):
        tower_tile, plate_tile = places(entry)[:2]
        c = at % per_tile * 2
        for r in parts:
            total = grad_feat[plate_tile, r]
            for n, block in enumerate(blocks_of(at)):
                back = back_buf[at % 2 * 2 + n, r]
                low = slice(width + r.start, width + r.stop)
                both_buf[block, r] = (back * gate_buf[block, r]).astype(BF16)
                both_buf[block, low] = (back * soft_buf[block, r]).astype(BF16)
                total = total + filt_buf[at % 2 * 2 + n, r] * adj_wide[tower_tile, c + n, r]
            grad_feat[plate_tile, r] = total
        for n, block in enumerate(blocks_of(at)):
            inner_buf[block] = back_buf[at % 2 * 2 + n, width : width + 8]

    def radial_stage(at, entry):
        tile, c = at // per_tile % 2, at % per_tile * 2
        lhs = jnp.concatenate([lhs_d[0], lhs_d[1]], axis=1)
        d_basis = nn(lhs, wide(both_buf, blocks_of(at)))
        for n, block in enumerate(blocks_of(at)):
            part = d_basis[:, n * LANES : (n + 1) * LANES]
            direct = jnp.sum(part[:nbasis] * slant_buf[block], axis=0, keepdims=True)
            inner = jnp.sum(inner_buf[block], axis=0, keepdims=True)
            inner = inner - math.log(2.0) * part[nbasis : nbasis + 1]
            pull_buf[c + n : c + n + 1] = direct + geo_row(at, 3)[n] * inner
        whole = blocks_of(at)
        acc_wf[...] += nt(wide(stack_buf, whole), wide(pair_buf, whole))
        acc_wr[...] += nt(wide(basis_buf, whole), wide(both_buf, whole, slice(0, width)))
        if at % per_tile < per_tile - 1:
            return
        _, _, recv_at, send_at, _ = places(entry)
        radial = pull_buf[...] * geo_buf[tile, 4]
        for axis in range(3):
            pull = geo_buf[tile, axis] * radial
            grad_recv[recv_at[0], recv_at[1], axis * rows + recv_at[2]] += pull
            grad_send[send_at[0], send_at[1], axis * rows + send_at[2]] += pull

    parts = [slice(r, r + PART) for r in range(0, width, PART)]
    for ref in (soft_buf, gate_buf):
        ref[2 * ring - 2 :] = jnp.zeros((2, *ref.shape[1:]), ref.dtype)
    for ref in (basis_buf, slant_buf, stack_buf, pair_buf, both_buf, inner_buf):
        ref[ring:] = jnp.zeros((ring, *ref.shape[1:]), ref.dtype)
    for ref in (back_buf, filt_buf, pull_buf):
        ref[...] = jnp.zeros_like(ref)
    geo_buf[1] = jnp.zeros(geo_buf.shape[1:], F32)
    geometry(0, 0)
    basis_stage(0)
    soft_stage(0, 0)
    basis_stage(1)

    def visit(step, carry):
        def entry_of(at):
            return jnp.maximum(2 * step + at // per_tile, 0)

        for at in range(ring):
            radial_stage(at - 2, entry_of(at - 2))
            feature_stage(at - 1, entry_of(at - 1))
            if at % per_tile == 1:
                geometry(entry_of(at) + 1, (at // per_tile + 1) % 2)
            product_stage(at)
            soft_stage(at + 1, entry_of(at + 1))
            basis_stage(at + 2)
        return carry

    steps = (count + 1) // 2
    lax.fori_loop(0, steps, visit, 0)
    last = 2 * steps - 1
    radial_stage(-2, last)
    feature_stage(-1, last)
    radial_stage(-1, last)

    digit = iota((1, width), 1)
    count_row = jnp.where(digit == 0, lax.rem(count, 16), 0)
    count_row = jnp.where(digit == 1, count // 16, count_row).astype(F32)
    weights = jnp.concatenate(
        [
            acc_wf[:width],
            acc_wr[:nbasis],
            acc_wf[width : width + 1],
            acc_wr[nbasis : nbasis + 1],
            count_row,
            jnp.zeros((weight_out.shape[0] - width - nbasis - 3, width), F32),
        ],
        axis=0,
    )
    weight_out[...] = weights
    put_split(send_out, weights)

    fold = one_hot(iota((TILE, LANES), 0) == iota((TILE, LANES), 1) % TILE)
    same_slot = one_hot(iota((LANES, LANES), 0) % TILE == iota((LANES, LANES), 1) % TILE)
    same_group = one_hot(iota((LANES, LANES), 0) // TILE == iota((LANES, LANES), 1) % groups)
    group_of = iota((spots, LANES), 1) // TILE
    padding = jnp.zeros((block_rows - atoms - spots, LANES), F32)
    for step in range(plate_count):
        brick = plate_at ^ step
        at = step // 2 * block_rows
        target = send_out if step % 2 else keep_out
        kind = target.dtype

        def fold_feat(half, carry, brick=brick, at=at, target=target, kind=kind):
            for t in range(4):
                t = 4 * half + t
                pieces = split(grad_feat[brick * per_brick + t], 2)
                start = pl.multiple_of(at + t * TILE, 16)
                target[pl.ds(start, TILE), :] = (
                    nt(fold, pieces[0]) + nt(fold, pieces[1])
                ).astype(kind)
            return carry

        lax.fori_loop(0, per_brick // 4, fold_feat, 0)
        total = jnp.zeros((spots, LANES), F32)
        for q in range(groups):
            summed = nn_split(jnp.sum(grad_send[brick, q], axis=1), same_slot)
            total = jnp.where(group_of == q, -summed, total)
        total = jnp.concatenate([total, padding], axis=0)
        target[at + atoms : at + block_rows] = total.astype(kind)
    lane = iota((chunks, LANES), 1)
    own_chunk = (lane // groups) % chunks == iota((chunks, LANES), 0)
    for target, slot in ((far_out, far_slot), (None, 1), (near_out, near_slot)):
        total = jnp.zeros((spots, chunks, LANES), F32)
        for q in range(groups):
            summed = nn_split(grad_recv[slot, q].reshape(spots * chunks, LANES), same_group)
            chosen = own_chunk & (lane // TILE == q)
            total = total + jnp.where(chosen[None], summed.reshape(spots, chunks, LANES), 0.0)
        total = jnp.concatenate([jnp.sum(total, axis=1), padding], axis=0)
        if target is None:
            keep_out[atoms:block_rows] += total
        else:
            target[...] = total


def put_split(target, weights):
    count = weights.shape[0]
    end = target.shape[0]
    high, low = split(weights, 2)
    target[end - 2 * count : end - count] = high
    target[end - count :] = low


def add_kernel(cut, kept_ref, weight_ref, got_ref, kept_out, send_out, weight_out):
    held, count = kept_ref.shape[0], weight_ref.shape[0]
    got = got_ref[...].astype(F32)
    total = kept_ref[...] + got[:held]
    weights = weight_ref[...] + got[held : held + count] + got[held + count :]
    kept_out[...] = total[:cut]
    send_out[: held - cut] = total[cut:].astype(BF16)
    put_split(send_out, weights)
    weight_out[...] = weights


def join_kernel(weight_ref, got_ref, near_ref, both_ref, weight_out, near_out):
    count = weight_ref.shape[0]
    start = got_ref.shape[0] - 2 * count
    got = got_ref[start:].astype(F32)
    weights = weight_ref[...] + got[:count] + got[count:]
    weight_out[...] = weights + (near_ref[:count] + both_ref[...])
    near_out[...] = near_ref[count:]


def finish_kernel(atoms, count_ref, block_ref, got_ref, near_ref, far_ref, feat_out, pos_out):
    block, width = block_ref.shape
    live = iota((atoms, width), 0) < count_ref[0, 0]
    total = block_ref[...] + got_ref[:block].astype(F32)
    feat_out[0] = jnp.where(live, total[:atoms], 0.0)
    spots = total[atoms:] + near_ref[...] + far_ref[...]
    rows = atoms // LANES
    for axis in range(3):
        for r in range(rows):
            at = axis * rows + r
            pos_out[axis, :, r * LANES : (r + 1) * LANES] = spots[at : at + 1]


def weight_kernel(*refs):
    ins, outs = refs[:-4], refs[-4:]
    total = ins[0][...]
    for other in ins[1:]:
        total = total + other[...]
    nbasis, width = outs[0].shape
    row = total[width + nbasis + 2 : width + nbasis + 3]
    tiles = row[:, :1] + 16.0 * row[:, 1:2]
    scale = lax.rsqrt(tiles * (TILE * TILE))
    outs[0][...] = total[width : width + nbasis] * scale
    outs[1][...] = total[width + nbasis + 1 : width + nbasis + 2] * scale
    outs[2][...] = total[:width] * scale
    outs[3][...] = total[width + nbasis : width + nbasis + 1] * scale


def swap(value, axis, route):
    size = lax.axis_size(axis)
    return lax.ppermute(value, axis, [(i, route(i) % size) for i in range(size)])


def across(bits):
    return lambda i: i ^ bits


def beyond(i):
    return i + 1 if i % 2 else i - 1


VMEM = pl.BlockSpec(memory_space=pltpu.VMEM)
SMEM = pl.BlockSpec(memory_space=pltpu.SMEM)


def call(kernel, shapes, places, **extra):
    return pl.pallas_call(
        kernel,
        out_shape=[jax.ShapeDtypeStruct(shape, kind) for shape, kind in shapes],
        in_specs=places,
        out_specs=[VMEM] * len(shapes),
        **extra,
    )


def local(
    features,
    adjoint,
    positions,
    w_rbf,
    b_rbf,
    w_filter,
    b_filter,
    atom_counts,
    tile_counts,
    tower_tiles,
    plate_tiles,
    image_shifts,
):
    atoms, width = features.shape[1:]
    nbasis = w_rbf.shape[0]
    per_brick = atoms // TILE
    groups = LANES // TILE
    chunks = TILE // groups
    plate_count = lax.axis_size("plate")
    tower_count = lax.axis_size("tower")
    if min(plate_count // 4, tower_count // 2) < 1 or any(
        size & (size - 1) for size in (plate_count, tower_count)
    ):
        raise ValueError("axis sizes")
    spots = 3 * (atoms // LANES)
    spot_rows = up(spots, 16)
    block = atoms + spot_rows
    weight_rows = up(width + nbasis + 3, 16)

    feat_block, adj_block = call(
        pack_kernel, [((block, width), BF16)] * 2, [SMEM, VMEM, VMEM, VMEM]
    )(atom_counts, features, adjoint, positions.astype(F32))
    peers = [swap(feat_block, "plate", across(step)) for step in range(1, plate_count)]
    near_adj = swap(adj_block, "tower", across(1))
    far_adj = swap(adj_block, "tower", beyond)

    at = jnp.stack([lax.axis_index("tower"), lax.axis_index("plate")]).astype(jnp.int32)
    half = plate_count // 2
    keep, send, weights, near_pos, far_pos = call(
        functools.partial(tile_kernel, plate_count),
        [
            ((half * block, width), F32),
            ((half * block + 2 * weight_rows, width), BF16),
            ((weight_rows, width), F32),
            ((spot_rows, width), F32),
            ((spot_rows, width), F32),
        ],
        [SMEM] * 5 + [VMEM] * (3 + plate_count + 4),
        scratch_shapes=[
            pltpu.VMEM((3 * per_brick, chunks, width, LANES), F32),
            pltpu.VMEM((plate_count * per_brick, width, LANES), F32),
            pltpu.VMEM((3, groups, spots, chunks, LANES), F32),
            pltpu.VMEM((plate_count, groups, spot_rows, LANES), F32),
            pltpu.VMEM((plate_count * per_brick, width, LANES), F32),
            pltpu.VMEM((3, groups, spots, chunks, LANES), F32),
            pltpu.VMEM((plate_count, groups, spots, chunks, LANES), F32),
            pltpu.VMEM((width + 16, width), F32),
            pltpu.VMEM((2 * nbasis, width), F32),
            pltpu.VMEM((width, 2 * nbasis), BF16),
            pltpu.VMEM((2, width, width), BF16),
            pltpu.VMEM((width + 16, width), BF16),
            pltpu.VMEM((2, 2 * nbasis, width), BF16),
        ]
        + [
            pltpu.VMEM((2 * chunks, width + 16, LANES), BF16),
            pltpu.VMEM((2 * chunks, width, LANES), F32),
            pltpu.VMEM((2 * chunks, width, LANES), F32),
            pltpu.VMEM((2 * chunks, width, LANES), BF16),
            pltpu.VMEM((2 * chunks, 2 * width, LANES), BF16),
            pltpu.VMEM((2 * chunks, 2 * nbasis, LANES), BF16),
            pltpu.VMEM((2 * chunks, nbasis, LANES), F32),
            pltpu.VMEM((2 * chunks, 8, LANES), F32),
            pltpu.VMEM((2, 7, chunks, LANES), F32),
            pltpu.VMEM((chunks, LANES), F32),
            pltpu.VMEM((4, width, LANES), F32),
            pltpu.VMEM((4, width + 16, LANES), F32),
            pltpu.VMEM((4, width, LANES), F32),
        ],
    )(
        at,
        tile_counts,
        tower_tiles,
        plate_tiles,
        image_shifts,
        adj_block,
        near_adj,
        far_adj,
        feat_block,
        *peers,
        w_rbf,
        b_rbf[None],
        w_filter,
        b_filter[None],
    )

    got_far = swap(far_pos, "tower", beyond)
    for step in [1] + [1 << n for n in range(plate_count.bit_length() - 2, 1, -1)]:
        got = swap(send, "plate", across(step))
        held = keep.shape[0]
        cut = held // 2
        keep, send, weights = call(
            functools.partial(add_kernel, cut),
            [
                ((cut, width), F32),
                ((held - cut + 2 * weight_rows, width), BF16),
                ((weight_rows, width), F32),
            ],
            [VMEM] * 3,
        )(keep, weights, got)
    both = swap(weights, ("tower", "plate"), across(plate_count + 2))
    near = swap(jnp.concatenate([weights, near_pos], axis=0), "tower", across(1))
    got = swap(send, "plate", across(2))
    weights, got_near = call(
        join_kernel, [((weight_rows, width), F32), ((spot_rows, width), F32)], [VMEM] * 4
    )(weights, got, near, both)

    bits = 2
    parts = [weights]
    while bits < tower_count:
        weights = sum(parts[1:], parts[0])
        stride = [s * bits for s in (1, 2, 3) if s * bits < tower_count]
        parts = [weights] + [swap(weights, "tower", across(s)) for s in stride]
        bits *= 4
    grad_features, grad_positions = call(
        functools.partial(finish_kernel, atoms),
        [((1, atoms, width), F32), ((3, 1, atoms), F32)],
        [SMEM] + [VMEM] * 4,
    )(atom_counts, keep, got, got_near, got_far)
    out_wr, out_br, out_wf, out_bf = call(
        weight_kernel,
        [((nbasis, width), F32), ((1, width), F32), ((width, width), F32), ((1, width), F32)],
        [VMEM] * len(parts),
    )(*parts)
    return grad_features, grad_positions, out_wr, out_br[0], out_wf, out_bf[0]


def solution(mesh):
    in_specs = (
        P("tower", "plate", None),
        P("tower", "plate", None),
        P(None, "tower", "plate"),
        P(),
        P(),
        P(),
        P(),
        P("tower", "plate"),
        P("tower", "plate"),
        P("tower", "plate", None),
        P("tower", "plate", None),
        P("tower", "plate", None),
    )
    out_specs = (P("tower", "plate", None), P(None, "tower", "plate"), P(), P(), P(), P())
    return jax.shard_map(local, mesh=mesh, in_specs=in_specs, out_specs=out_specs, check_vma=False)
```

```python
import functools
import math

import jax
import jax.numpy as jnp
from jax import lax
from jax.experimental import pallas as pl
from jax.experimental.pallas import tpu as pltpu
from jax.sharding import PartitionSpec as P


TILE = 32
LANES = 128
PART = 32
TILES = 4

box_side = 1.0
brick_height = 1.0
cutoff_radius = 3.0
soften = 0.01
sharpness = 10.0

F32 = jnp.float32
BF16 = jnp.bfloat16


def up(value, unit):
    return -(-value // unit) * unit


def iota(shape, axis):
    return lax.broadcasted_iota(jnp.int32, shape, axis)


def one_hot(cond):
    return jnp.where(cond, 1.0, 0.0).astype(BF16)


def nn(left, right):
    return lax.dot_general(left, right, (((1,), (0,)), ((), ())), preferred_element_type=F32)


def nt(left, right):
    return lax.dot_general(left, right, (((1,), (1,)), ((), ())), preferred_element_type=F32)


def split(value, parts):
    pieces = []
    for _ in range(parts):
        piece = value.astype(BF16)
        pieces.append(piece)
        value = value - piece.astype(F32)
    return pieces


def nn_split(left, right):
    pieces = split(left, 2)
    return nn(pieces[0], right) + nn(pieces[1], right)


def poly(square, coefs):
    total = jnp.full_like(square, coefs[-1])
    for coef in coefs[-2::-1]:
        total = total * square + coef
    return total


SIN = [(-1.0) ** n / math.factorial(2 * n + 1) for n in range(7)]
COS = [(-1.0) ** n / math.factorial(2 * n) for n in range(8)]


def pack_kernel(count_ref, feat_ref, adj_ref, pos_ref, out_feat, out_adj):
    atoms, width = feat_ref.shape[1:]
    live = iota((atoms, width), 0) < count_ref[0, 0]
    rows = atoms // LANES
    extra = out_feat.shape[0] - atoms
    parts = [
        pos_ref[axis, :, r * LANES : (r + 1) * LANES] for axis in range(3) for r in range(rows)
    ]
    parts.append(jnp.zeros((extra - len(parts), width), F32))
    tail = jnp.concatenate(parts, axis=0).astype(BF16)
    for source, target in ((feat_ref, out_feat), (adj_ref, out_adj)):
        kept = jnp.where(live, source[0].astype(F32), 0.0)
        target[:atoms] = kept.astype(BF16)
        target[atoms:] = tail


def tile_kernel(
    plate_count,
    where_ref,
    count_ref,
    tower_ref,
    plate_ref,
    shift_ref,
    *refs,
):
    (own_adj, near_adj, far_adj), refs = refs[:3], refs[3:]
    feats, refs = refs[:plate_count], refs[plate_count:]
    (w_rbf_ref, b_rbf_ref, w_filter_ref, b_filter_ref), refs = refs[:4], refs[4:]
    (keep_out, send_out, weight_out, near_out, far_out), refs = refs[:5], refs[5:]
    (
        adj_wide,
        feat_wide,
        recv_wide,
        send_wide,
        grad_feat,
        grad_recv,
        grad_send,
        acc_wf,
        acc_wr,
        lhs_x,
        lhs_f,
        lhs_a,
        lhs_d,
    ), refs = refs[:13], refs[13:]
    stack_buf, soft_buf, gate_buf, pair_buf, both_buf, refs = *refs[:5], refs[5:]
    basis_buf, slant_buf, inner_buf, geo_buf, pull_buf, *refs = refs
    half_buf, back_buf, filt_buf = refs
    width = w_filter_ref.shape[0]
    nbasis = w_rbf_ref.shape[0]
    block_rows = own_adj.shape[0]
    groups = LANES // TILE
    chunks = TILE // groups
    pairs = TILE * TILE
    per_brick = adj_wide.shape[0] // 3
    atoms = per_brick * TILE
    rows = atoms // LANES
    spots = 3 * rows
    tower_at = where_ref[0]
    plate_at = where_ref[1]
    odd = lax.rem(tower_at, 2)
    near_slot = 2 - 2 * odd
    far_slot = 2 * odd
    sources = ((far_adj, far_slot), (own_adj, 1), (near_adj, near_slot))

    pick_recv = one_hot(iota((TILE, pairs), 0) == iota((TILE, pairs), 1) // TILE)
    pick_send = one_hot(iota((TILE, LANES), 0) == iota((TILE, LANES), 1) % TILE)
    for source, slot in sources:

        def widen_adj(half, carry, source=source, slot=slot):
            for t in range(4):
                t = 4 * half + t
                start = pl.multiple_of(t * TILE, TILE)
                part = source[pl.ds(start, TILE), :].astype(F32).T.astype(BF16)
                wide = nn(part, pick_recv)
                for c in range(chunks):
                    adj_wide[slot * per_brick + t, c] = wide[:, c * LANES : (c + 1) * LANES]
            return carry

        lax.fori_loop(0, per_brick // 4, widen_adj, 0)
    for q in range(groups):
        pick = one_hot(iota((LANES, pairs), 0) == q * TILE + iota((LANES, pairs), 1) // TILE)
        for source, slot in sources:
            wide = nn(source[atoms:block_rows], pick)
            for c in range(chunks):
                recv_wide[slot, q, :, c, :] = wide[:spots, c * LANES : (c + 1) * LANES]
    for q in range(groups):
        pick = one_hot(iota((LANES, LANES), 0) == q * TILE + iota((LANES, LANES), 1) % TILE)
        for step, source in enumerate(feats):
            send_wide[plate_at ^ step, q] = nn(source[atoms:block_rows], pick)
    for step, source in enumerate(feats):
        brick = plate_at ^ step

        def widen_feat(half, carry, source=source, brick=brick):
            for t in range(4):
                t = 4 * half + t
                start = pl.multiple_of(t * TILE, TILE)
                part = source[pl.ds(start, TILE), :].astype(F32).T.astype(BF16)
                feat_wide[brick * per_brick + t] = nn(part, pick_send)
            return carry

        lax.fori_loop(0, per_brick // 4, widen_feat, 0)

    w_rbf = w_rbf_ref[...].astype(F32)
    half_bias = [piece.astype(F32) for piece in split(0.5 * b_rbf_ref[...], 3)]
    stacked = jnp.concatenate(
        [0.5 * w_rbf] + half_bias + [jnp.zeros((LANES - nbasis - 3, width), F32)], axis=0
    )
    lhs_x[...] = stacked.T[:, : 2 * nbasis].astype(BF16)
    w_filter = w_filter_ref[...].astype(F32)
    bias = [piece.astype(F32) for piece in split(b_filter_ref[...], 3)]
    bias = jnp.concatenate(bias + [jnp.zeros((LANES - 3, width), F32)], axis=0)
    lhs_f[0] = w_filter.T.astype(BF16)
    lhs_f[1] = bias.T.astype(BF16)
    lhs_a[:width] = w_filter_ref[...]
    lhs_a[width:] = bias[:16].astype(BF16)
    lhs_d[0, :nbasis] = w_rbf_ref[...]
    lhs_d[0, nbasis:] = jnp.zeros((nbasis, width), BF16)
    lhs_d[1, :nbasis] = jnp.zeros((nbasis, width), BF16)
    lhs_d[1, nbasis:] = one_hot(iota((nbasis, width), 0) == 0)

    grad_feat[...] = jnp.zeros_like(grad_feat)
    grad_recv[...] = jnp.zeros_like(grad_recv)
    grad_send[...] = jnp.zeros_like(grad_send)
    acc_wf[...] = jnp.zeros_like(acc_wf)
    acc_wr[...] = jnp.zeros_like(acc_wr)

    count = count_ref[0, 0]
    span = 2 * LANES
    centres = iota((nbasis, LANES), 0).astype(F32) * (cutoff_radius / (nbasis - 1))
    ones_rows = jnp.ones((nbasis, LANES), BF16)

    def places(entry):
        entry = jnp.minimum(entry, count - 1)
        tower_tile = tower_ref[0, 0, entry]
        plate_tile = plate_ref[0, 0, entry]
        recv_t = tower_tile % per_brick
        send_t = plate_tile % per_brick
        recv = (tower_tile // per_brick, recv_t % groups, recv_t // groups)
        send = (plate_tile // per_brick, send_t % groups, send_t // groups)
        return tower_tile, plate_tile, recv, send, shift_ref[0, 0, entry]

    per_tile = pairs // span
    ring = 2 * per_tile

    def blocks_of(at):
        return (at % ring * 2, at % ring * 2 + 1)

    def wide(ref, blocks, rows=slice(None)):
        return jnp.concatenate([ref[n, rows] for n in blocks], axis=1)

    def geometry(entry, tile):
        _, _, recv_at, send_at, code = places(entry)
        shifts = (
            (code // 3 - 1).astype(F32) * box_side,
            (code % 3 - 1).astype(F32) * box_side,
            (recv_at[0] - 1).astype(F32) * brick_height,
        )
        square = soften
        for axis in range(3):
            recv = recv_wide[recv_at[0], recv_at[1], axis * rows + recv_at[2]]
            send = send_wide[send_at[0], send_at[1], pl.ds(axis * rows + send_at[2], 1), :]
            disp = recv + shifts[axis] - send
            geo_buf[tile, axis] = disp
            square = square + disp * disp
        dist = jnp.sqrt(square)
        inside = dist < jnp.where(entry < count, cutoff_radius, 0.0)
        angle = (0.5 * math.pi / cutoff_radius) * (cutoff_radius - dist)
        square = angle * angle
        sine = angle * poly(square, SIN)
        cosine = poly(square, COS)
        geo_buf[tile, 3] = jnp.where(inside, (-math.pi / cutoff_radius) * sine * cosine, 0.0)
        geo_buf[tile, 4] = 1.0 / dist
        geo_buf[tile, 5] = dist
        geo_buf[tile, 6] = jnp.where(inside, sine * sine, 0.0)

    def geo_row(at, which):
        tile, c = at // per_tile % 2, at % per_tile * 2
        return [geo_buf[tile, which, n : n + 1] for n in (c, c + 1)]

    def basis_stage(at):
        for n, dist in zip(blocks_of(at), geo_row(at, 5)):
            offsets = dist - centres
            basis = jnp.exp(-sharpness * offsets * offsets)
            slant_buf[n] = (-2.0 * sharpness) * basis * offsets
            basis_buf[n] = jnp.concatenate([basis.astype(BF16), ones_rows], axis=0)
        half = nn(lhs_x[...], wide(basis_buf, blocks_of(at)))
        half_buf[at % 2 * 2] = half[:, :LANES]
        half_buf[at % 2 * 2 + 1] = half[:, LANES:]

    def soft_stage(at, entry):
        tower_tile, plate_tile = places(entry)[:2]
        c = at % per_tile * 2
        for n, block in enumerate(blocks_of(at)):
            env_rows = jnp.broadcast_to(geo_row(at, 6)[n], (PART, LANES))
            half_env = 0.5 * env_rows
            log_env = -math.log(2.0) * env_rows
            stack_buf[block, width:] = env_rows[:16].astype(BF16)
            for r in parts:
                tanh = jnp.tanh(half_buf[at % 2 * 2 + n, r])
                soft = jnp.log2(1.0 - tanh)
                soft_buf[block, r] = soft
                stack_buf[block, r] = (soft * log_env).astype(BF16)
                gate_buf[block, r] = (tanh + 1.0) * half_env
                pair = adj_wide[tower_tile, c + n, r] * feat_wide[plate_tile, r]
                pair_buf[block, r] = pair.astype(BF16)

    def product_stage(at):
        blocks = blocks_of(at)
        back = nn(lhs_a[...], wide(pair_buf, blocks))
        lhs = jnp.concatenate([lhs_f[0], lhs_f[1, :, :16]], axis=1)
        filt = nn(lhs, wide(stack_buf, blocks))
        for n in range(2):
            back_buf[at % 2 * 2 + n] = back[:, n * LANES : (n + 1) * LANES]
            filt_buf[at % 2 * 2 + n] = filt[:, n * LANES : (n + 1) * LANES]

    def feature_stage(at, entry):
        tower_tile, plate_tile = places(entry)[:2]
        c = at % per_tile * 2
        for r in parts:
            total = grad_feat[plate_tile, r]
            for n, block in enumerate(blocks_of(at)):
                back = back_buf[at % 2 * 2 + n, r]
                low = slice(width + r.start, width + r.stop)
                both_buf[block, r] = (back * gate_buf[block, r]).astype(BF16)
                both_buf[block, low] = (back * soft_buf[block, r]).astype(BF16)
                total = total + filt_buf[at % 2 * 2 + n, r] * adj_wide[tower_tile, c + n, r]
            grad_feat[plate_tile, r] = total
        for n, block in enumerate(blocks_of(at)):
            inner_buf[block] = back_buf[at % 2 * 2 + n, width : width + 8]

    def radial_stage(at, entry):
        tile, c = at // per_tile % 2, at % per_tile * 2
        lhs = jnp.concatenate([lhs_d[0], lhs_d[1]], axis=1)
        d_basis = nn(lhs, wide(both_buf, blocks_of(at)))
        for n, block in enumerate(blocks_of(at)):
            part = d_basis[:, n * LANES : (n + 1) * LANES]
            direct = jnp.sum(part[:nbasis] * slant_buf[block], axis=0, keepdims=True)
            inner = jnp.sum(inner_buf[block], axis=0, keepdims=True)
            inner = inner - math.log(2.0) * part[nbasis : nbasis + 1]
            pull_buf[c + n : c + n + 1] = direct + geo_row(at, 3)[n] * inner
        whole = blocks_of(at)
        acc_wf[...] += nt(wide(stack_buf, whole), wide(pair_buf, whole))
        acc_wr[...] += nt(wide(basis_buf, whole), wide(both_buf, whole, slice(0, width)))
        if at % per_tile < per_tile - 1:
            return
        _, _, recv_at, send_at, _ = places(entry)
        radial = pull_buf[...] * geo_buf[tile, 4]
        for axis in range(3):
            pull = geo_buf[tile, axis] * radial
            grad_recv[recv_at[0], recv_at[1], axis * rows + recv_at[2]] += pull
            grad_send[send_at[0], send_at[1], axis * rows + send_at[2]] += pull

    parts = [slice(r, r + PART) for r in range(0, width, PART)]
    for ref in (soft_buf, gate_buf):
        ref[2 * ring - 2 :] = jnp.zeros((2, *ref.shape[1:]), ref.dtype)
    for ref in (basis_buf, slant_buf, stack_buf, pair_buf, both_buf, inner_buf):
        ref[2 * ring - 4 :] = jnp.zeros((4, *ref.shape[1:]), ref.dtype)
    for ref in (back_buf, filt_buf, pull_buf):
        ref[...] = jnp.zeros_like(ref)
    geo_buf[1] = jnp.zeros(geo_buf.shape[1:], F32)
    geometry(0, 0)
    basis_stage(0)
    soft_stage(0, 0)
    basis_stage(1)

    def visit(step, carry):
        def entry_of(at):
            return jnp.maximum(TILES * step + at // per_tile, 0)

        for at in range(TILES * per_tile):
            radial_stage(at - 2, entry_of(at - 2))
            feature_stage(at - 1, entry_of(at - 1))
            if at % per_tile == 1:
                geometry(entry_of(at) + 1, (at // per_tile + 1) % 2)
            product_stage(at)
            soft_stage(at + 1, entry_of(at + 1))
            basis_stage(at + 2)
        return carry

    steps = (count + TILES - 1) // TILES
    lax.fori_loop(0, steps, visit, 0)
    last = TILES * steps - 1
    radial_stage(-2, last)
    feature_stage(-1, last)
    radial_stage(-1, last)

    digit = iota((1, width), 1)
    count_row = jnp.where(digit == 0, lax.rem(count, 16), 0)
    count_row = jnp.where(digit == 1, count // 16, count_row).astype(F32)
    weights = jnp.concatenate(
        [
            acc_wf[:width],
            acc_wr[:nbasis],
            acc_wf[width : width + 1],
            acc_wr[nbasis : nbasis + 1],
            count_row,
            jnp.zeros((weight_out.shape[0] - width - nbasis - 3, width), F32),
        ],
        axis=0,
    )
    weight_out[...] = weights
    put_split(send_out, weights)

    fold = one_hot(iota((TILE, LANES), 0) == iota((TILE, LANES), 1) % TILE)
    same_slot = one_hot(iota((LANES, LANES), 0) % TILE == iota((LANES, LANES), 1) % TILE)
    same_group = one_hot(iota((LANES, LANES), 0) // TILE == iota((LANES, LANES), 1) % groups)
    group_of = iota((spots, LANES), 1) // TILE
    padding = jnp.zeros((block_rows - atoms - spots, LANES), F32)
    for step in range(plate_count):
        brick = plate_at ^ step
        at = step // 2 * block_rows
        target = send_out if step % 2 else keep_out
        kind = target.dtype

        def fold_feat(half, carry, brick=brick, at=at, target=target, kind=kind):
            for t in range(4):
                t = 4 * half + t
                pieces = split(grad_feat[brick * per_brick + t], 2)
                start = pl.multiple_of(at + t * TILE, 16)
                target[pl.ds(start, TILE), :] = (
                    nt(fold, pieces[0]) + nt(fold, pieces[1])
                ).astype(kind)
            return carry

        lax.fori_loop(0, per_brick // 4, fold_feat, 0)
        total = jnp.zeros((spots, LANES), F32)
        for q in range(groups):
            summed = nn_split(jnp.sum(grad_send[brick, q], axis=1), same_slot)
            total = jnp.where(group_of == q, -summed, total)
        total = jnp.concatenate([total, padding], axis=0)
        target[at + atoms : at + block_rows] = total.astype(kind)
    lane = iota((chunks, LANES), 1)
    own_chunk = (lane // groups) % chunks == iota((chunks, LANES), 0)
    for target, slot in ((far_out, far_slot), (None, 1), (near_out, near_slot)):
        total = jnp.zeros((spots, chunks, LANES), F32)
        for q in range(groups):
            summed = nn_split(grad_recv[slot, q].reshape(spots * chunks, LANES), same_group)
            chosen = own_chunk & (lane // TILE == q)
            total = total + jnp.where(chosen[None], summed.reshape(spots, chunks, LANES), 0.0)
        total = jnp.concatenate([jnp.sum(total, axis=1), padding], axis=0)
        if target is None:
            keep_out[atoms:block_rows] += total
        else:
            target[...] = total


def put_split(target, weights):
    count = weights.shape[0]
    end = target.shape[0]
    high, low = split(weights, 2)
    target[end - 2 * count : end - count] = high
    target[end - count :] = low


def add_kernel(cut, kept_ref, weight_ref, got_ref, near_ref, kept_out, send_out, weight_out):
    held, count = kept_ref.shape[0], weight_out.shape[0] - near_ref.shape[0]
    got = got_ref[...].astype(F32)
    total = kept_ref[...] + got[:held]
    weights = weight_ref[:count] + got[held : held + count] + got[held + count :]
    kept_out[...] = total[:cut]
    send_out[: held - cut] = total[cut:].astype(BF16)
    put_split(send_out, weights)
    weight_out[:count] = weights
    weight_out[count:] = near_ref[...]


def join_kernel(weight_ref, got_ref, near_ref, both_ref, weight_out, near_out):
    count = weight_out.shape[0]
    start = got_ref.shape[0] - 2 * count
    got = got_ref[start:].astype(F32)
    weights = weight_ref[:count] + got[:count] + got[count:]
    weight_out[...] = weights + (near_ref[:count] + both_ref[:count])
    near_out[...] = near_ref[count:]


def finish_kernel(atoms, count_ref, block_ref, got_ref, near_ref, far_ref, feat_out, pos_out):
    block, width = block_ref.shape
    live = iota((atoms, width), 0) < count_ref[0, 0]
    total = block_ref[...] + got_ref[:block].astype(F32)
    feat_out[0] = jnp.where(live, total[:atoms], 0.0)
    spots = total[atoms:] + near_ref[...] + far_ref[...]
    rows = atoms // LANES
    for axis in range(3):
        for r in range(rows):
            at = axis * rows + r
            pos_out[axis, :, r * LANES : (r + 1) * LANES] = spots[at : at + 1]


def weight_kernel(*refs):
    ins, outs = refs[:-4], refs[-4:]
    total = ins[0][...]
    for other in ins[1:]:
        total = total + other[...]
    nbasis, width = outs[0].shape
    row = total[width + nbasis + 2 : width + nbasis + 3]
    tiles = row[:, :1] + 16.0 * row[:, 1:2]
    scale = lax.rsqrt(tiles * (TILE * TILE))
    outs[0][...] = total[width : width + nbasis] * scale
    outs[1][...] = total[width + nbasis + 1 : width + nbasis + 2] * scale
    outs[2][...] = total[:width] * scale
    outs[3][...] = total[width + nbasis : width + nbasis + 1] * scale


def swap(value, axis, route):
    size = lax.axis_size(axis)
    return lax.ppermute(value, axis, [(i, route(i) % size) for i in range(size)])


def across(bits):
    return lambda i: i ^ bits


def beyond(i):
    return i + 1 if i % 2 else i - 1


VMEM = pl.BlockSpec(memory_space=pltpu.VMEM)
SMEM = pl.BlockSpec(memory_space=pltpu.SMEM)


def call(kernel, shapes, places, **extra):
    return pl.pallas_call(
        kernel,
        out_shape=[jax.ShapeDtypeStruct(shape, kind) for shape, kind in shapes],
        in_specs=places,
        out_specs=[VMEM] * len(shapes),
        **extra,
    )


def local(
    features,
    adjoint,
    positions,
    w_rbf,
    b_rbf,
    w_filter,
    b_filter,
    atom_counts,
    tile_counts,
    tower_tiles,
    plate_tiles,
    image_shifts,
):
    atoms, width = features.shape[1:]
    nbasis = w_rbf.shape[0]
    per_brick = atoms // TILE
    groups = LANES // TILE
    chunks = TILE // groups
    plate_count = lax.axis_size("plate")
    tower_count = lax.axis_size("tower")
    if min(plate_count // 4, tower_count // 2) < 1 or any(
        size & (size - 1) for size in (plate_count, tower_count)
    ):
        raise ValueError("axis sizes")
    spots = 3 * (atoms // LANES)
    spot_rows = up(spots, 16)
    block = atoms + spot_rows
    weight_rows = up(width + nbasis + 3, 16)

    feat_block, adj_block = call(
        pack_kernel, [((block, width), BF16)] * 2, [SMEM, VMEM, VMEM, VMEM]
    )(atom_counts, features, adjoint, positions.astype(F32))
    peers = [swap(feat_block, "plate", across(step)) for step in range(1, plate_count)]
    near_adj = swap(adj_block, "tower", across(1))
    far_adj = swap(adj_block, "tower", beyond)

    at = jnp.stack([lax.axis_index("tower"), lax.axis_index("plate")]).astype(jnp.int32)
    half = plate_count // 2
    keep, send, weights, near_pos, far_pos = call(
        functools.partial(tile_kernel, plate_count),
        [
            ((half * block, width), F32),
            ((half * block + 2 * weight_rows, width), BF16),
            ((weight_rows, width), F32),
            ((spot_rows, width), F32),
            ((spot_rows, width), F32),
        ],
        [SMEM] * 5 + [VMEM] * (3 + plate_count + 4),
        scratch_shapes=[
            pltpu.VMEM((3 * per_brick, chunks, width, LANES), F32),
            pltpu.VMEM((plate_count * per_brick, width, LANES), F32),
            pltpu.VMEM((3, groups, spots, chunks, LANES), F32),
            pltpu.VMEM((plate_count, groups, spot_rows, LANES), F32),
            pltpu.VMEM((plate_count * per_brick, width, LANES), F32),
            pltpu.VMEM((3, groups, spots, chunks, LANES), F32),
            pltpu.VMEM((plate_count, groups, spots, chunks, LANES), F32),
            pltpu.VMEM((width + 16, width), F32),
            pltpu.VMEM((2 * nbasis, width), F32),
            pltpu.VMEM((width, 2 * nbasis), BF16),
            pltpu.VMEM((2, width, width), BF16),
            pltpu.VMEM((width + 16, width), BF16),
            pltpu.VMEM((2, 2 * nbasis, width), BF16),
        ]
        + [
            pltpu.VMEM((2 * chunks, width + 16, LANES), BF16),
            pltpu.VMEM((2 * chunks, width, LANES), F32),
            pltpu.VMEM((2 * chunks, width, LANES), F32),
            pltpu.VMEM((2 * chunks, width, LANES), BF16),
            pltpu.VMEM((2 * chunks, 2 * width, LANES), BF16),
            pltpu.VMEM((2 * chunks, 2 * nbasis, LANES), BF16),
            pltpu.VMEM((2 * chunks, nbasis, LANES), F32),
            pltpu.VMEM((2 * chunks, 8, LANES), F32),
            pltpu.VMEM((2, 7, chunks, LANES), F32),
            pltpu.VMEM((chunks, LANES), F32),
            pltpu.VMEM((4, width, LANES), F32),
            pltpu.VMEM((4, width + 16, LANES), F32),
            pltpu.VMEM((4, width, LANES), F32),
        ],
    )(
        at,
        tile_counts,
        tower_tiles,
        plate_tiles,
        image_shifts,
        adj_block,
        near_adj,
        far_adj,
        feat_block,
        *peers,
        w_rbf,
        b_rbf[None],
        w_filter,
        b_filter[None],
    )

    got_far = swap(far_pos, "tower", beyond)
    for step in [1] + [1 << n for n in range(plate_count.bit_length() - 2, 1, -1)]:
        got = swap(send, "plate", across(step))
        held = keep.shape[0]
        cut = held // 2
        keep, send, weights = call(
            functools.partial(add_kernel, cut),
            [
                ((cut, width), F32),
                ((held - cut + 2 * weight_rows, width), BF16),
                ((weight_rows + spot_rows, width), F32),
            ],
            [VMEM] * 4,
        )(keep, weights, got, near_pos)
    both = swap(weights, ("tower", "plate"), across(plate_count + 2))
    near = swap(weights, "tower", across(1))
    got = swap(send, "plate", across(2))
    weights, got_near = call(
        join_kernel, [((weight_rows, width), F32), ((spot_rows, width), F32)], [VMEM] * 4
    )(weights, got, near, both)

    bits = 2
    parts = [weights]
    while bits < tower_count:
        weights = sum(parts[1:], parts[0])
        stride = [s * bits for s in (1, 2, 3) if s * bits < tower_count]
        parts = [weights] + [swap(weights, "tower", across(s)) for s in stride]
        bits *= 4
    grad_features, grad_positions = call(
        functools.partial(finish_kernel, atoms),
        [((1, atoms, width), F32), ((3, 1, atoms), F32)],
        [SMEM] + [VMEM] * 4,
    )(atom_counts, keep, got, got_near, got_far)
    out_wr, out_br, out_wf, out_bf = call(
        weight_kernel,
        [((nbasis, width), F32), ((1, width), F32), ((width, width), F32), ((1, width), F32)],
        [VMEM] * len(parts),
    )(*parts)
    return grad_features, grad_positions, out_wr, out_br[0], out_wf, out_bf[0]


def solution(mesh):
    in_specs = (
        P("tower", "plate", None),
        P("tower", "plate", None),
        P(None, "tower", "plate"),
        P(),
        P(),
        P(),
        P(),
        P("tower", "plate"),
        P("tower", "plate"),
        P("tower", "plate", None),
        P("tower", "plate", None),
        P("tower", "plate", None),
    )
    out_specs = (P("tower", "plate", None), P(None, "tower", "plate"), P(), P(), P(), P())
    return jax.shard_map(local, mesh=mesh, in_specs=in_specs, out_specs=out_specs, check_vma=False)
```

```python
import functools
import math

import jax
import jax.numpy as jnp
from jax import lax
from jax.experimental import pallas as pl
from jax.experimental.pallas import tpu as pltpu
from jax.sharding import PartitionSpec as P


TILE = 32
LANES = 128
PART = 32
TILES = 8

box_side = 1.0
brick_height = 1.0
cutoff_radius = 3.0
soften = 0.01
sharpness = 10.0

F32 = jnp.float32
BF16 = jnp.bfloat16


def up(value, unit):
    return -(-value // unit) * unit


def iota(shape, axis):
    return lax.broadcasted_iota(jnp.int32, shape, axis)


def one_hot(cond):
    return jnp.where(cond, 1.0, 0.0).astype(BF16)


def nn(left, right):
    return lax.dot_general(left, right, (((1,), (0,)), ((), ())), preferred_element_type=F32)


def nt(left, right):
    return lax.dot_general(left, right, (((1,), (1,)), ((), ())), preferred_element_type=F32)


def split(value, parts):
    pieces = []
    for _ in range(parts):
        piece = value.astype(BF16)
        pieces.append(piece)
        value = value - piece.astype(F32)
    return pieces


def nn_split(left, right):
    pieces = split(left, 2)
    return nn(pieces[0], right) + nn(pieces[1], right)


def poly(square, coefs):
    total = jnp.full_like(square, coefs[-1])
    for coef in coefs[-2::-1]:
        total = total * square + coef
    return total


SIN = [(-1.0) ** n / math.factorial(2 * n + 1) for n in range(7)]
COS = [(-1.0) ** n / math.factorial(2 * n) for n in range(8)]


def pack_kernel(count_ref, feat_ref, adj_ref, pos_ref, out_feat, out_adj):
    atoms, width = feat_ref.shape[1:]
    live = iota((atoms, width), 0) < count_ref[0, 0]
    rows = atoms // LANES
    extra = out_feat.shape[0] - atoms
    spots = pos_ref[...].astype(F32)
    parts = [
        spots[axis : axis + 1, r * LANES : (r + 1) * LANES]
        for axis in range(3)
        for r in range(rows)
    ]
    parts.append(jnp.zeros((extra - len(parts), width), F32))
    tail = jnp.concatenate(parts, axis=0).astype(BF16)
    for source, target in ((feat_ref, out_feat), (adj_ref, out_adj)):
        kept = jnp.where(live, source[0].astype(F32), 0.0)
        target[:atoms] = kept.astype(BF16)
        target[atoms:] = tail


def tile_kernel(
    plate_count,
    where_ref,
    count_ref,
    tower_ref,
    plate_ref,
    shift_ref,
    *refs,
):
    (own_adj, near_adj, far_adj), refs = refs[:3], refs[3:]
    feats, refs = refs[:plate_count], refs[plate_count:]
    (w_rbf_ref, b_rbf_ref, w_filter_ref, b_filter_ref), refs = refs[:4], refs[4:]
    (keep_out, send_out, weight_out, near_out, far_out), refs = refs[:5], refs[5:]
    (
        adj_wide,
        feat_wide,
        recv_wide,
        send_wide,
        grad_feat,
        grad_recv,
        grad_send,
        acc_wf,
        acc_wr,
        lhs_x,
        lhs_f,
        lhs_a,
        lhs_d,
    ), refs = refs[:13], refs[13:]
    stack_buf, soft_buf, gate_buf, pair_buf, both_buf, refs = *refs[:5], refs[5:]
    basis_buf, slant_buf, inner_buf, geo_buf, pull_buf, *refs = refs
    half_buf, back_buf, filt_buf = refs
    width = w_filter_ref.shape[0]
    nbasis = w_rbf_ref.shape[0]
    block_rows = own_adj.shape[0]
    groups = LANES // TILE
    chunks = TILE // groups
    pairs = TILE * TILE
    per_brick = adj_wide.shape[0] // 3
    atoms = per_brick * TILE
    rows = atoms // LANES
    spots = 3 * rows
    tower_at = where_ref[0]
    plate_at = where_ref[1]
    odd = lax.rem(tower_at, 2)
    near_slot = 2 - 2 * odd
    far_slot = 2 * odd
    sources = ((far_adj, far_slot), (own_adj, 1), (near_adj, near_slot))

    pick_send = one_hot(iota((TILE, LANES), 0) == iota((TILE, LANES), 1) % TILE)
    for source, slot in sources:
        for half in range(rows):
            turned = source[half * LANES : (half + 1) * LANES].astype(F32).T
            for q in range(groups):
                for c in range(chunks):
                    lane = q * TILE + c * groups + iota((width, LANES), 1) // TILE
                    adj_wide[slot * per_brick + half * groups + q, c] = jnp.take_along_axis(
                        turned, lane, axis=1
                    )
    for q in range(groups):
        pick = one_hot(iota((LANES, pairs), 0) == q * TILE + iota((LANES, pairs), 1) // TILE)
        for source, slot in sources:
            wide = nn(source[atoms:block_rows], pick)
            for c in range(chunks):
                recv_wide[slot, q, :, c, :] = wide[:spots, c * LANES : (c + 1) * LANES]
    for q in range(groups):
        pick = one_hot(iota((LANES, LANES), 0) == q * TILE + iota((LANES, LANES), 1) % TILE)
        for step, source in enumerate(feats):
            send_wide[plate_at ^ step, q] = nn(source[atoms:block_rows], pick)
    for step, source in enumerate(feats):
        brick = plate_at ^ step

        def widen_feat(half, carry, source=source, brick=brick):
            for t in range(per_brick):
                start = pl.multiple_of(t * TILE, TILE)
                part = source[pl.ds(start, TILE), :].astype(F32).T.astype(BF16)
                feat_wide[brick * per_brick + t] = nn(part, pick_send)
            return carry

        lax.fori_loop(0, 1, widen_feat, 0)

    w_rbf = w_rbf_ref[...].astype(F32)
    half_bias = [piece.astype(F32) for piece in split(0.5 * b_rbf_ref[...], 3)]
    stacked = jnp.concatenate(
        [0.5 * w_rbf] + half_bias + [jnp.zeros((LANES - nbasis - 3, width), F32)], axis=0
    )
    lhs_x[...] = stacked.T[:, : 2 * nbasis].astype(BF16)
    w_filter = w_filter_ref[...].astype(F32)
    bias = [piece.astype(F32) for piece in split(b_filter_ref[...], 3)]
    bias = jnp.concatenate(bias + [jnp.zeros((LANES - 3, width), F32)], axis=0)
    lhs_f[0] = w_filter.T.astype(BF16)
    lhs_f[1] = bias.T.astype(BF16)
    lhs_a[:width] = w_filter_ref[...]
    lhs_a[width:] = bias[:16].astype(BF16)
    lhs_d[0, :nbasis] = w_rbf_ref[...]
    lhs_d[0, nbasis:] = jnp.zeros((nbasis, width), BF16)
    lhs_d[1, :nbasis] = jnp.zeros((nbasis, width), BF16)
    lhs_d[1, nbasis:] = one_hot(iota((nbasis, width), 0) == 0)

    grad_feat[...] = jnp.zeros_like(grad_feat)
    grad_recv[...] = jnp.zeros_like(grad_recv)
    grad_send[...] = jnp.zeros_like(grad_send)
    acc_wf[...] = jnp.zeros_like(acc_wf)
    acc_wr[...] = jnp.zeros_like(acc_wr)

    count = count_ref[0, 0]
    span = 2 * LANES
    centres = iota((nbasis, LANES), 0).astype(F32) * (cutoff_radius / (nbasis - 1))
    ones_rows = jnp.ones((nbasis, LANES), BF16)

    def places(entry):
        entry = jnp.minimum(entry, count - 1)
        tower_tile = tower_ref[0, 0, entry]
        plate_tile = plate_ref[0, 0, entry]
        recv_t = tower_tile % per_brick
        send_t = plate_tile % per_brick
        recv = (tower_tile // per_brick, recv_t % groups, recv_t // groups)
        send = (plate_tile // per_brick, send_t % groups, send_t // groups)
        return tower_tile, plate_tile, recv, send, shift_ref[0, 0, entry]

    per_tile = pairs // span
    ring = 2 * per_tile

    def blocks_of(at):
        return (at % ring * 2, at % ring * 2 + 1)

    def wide(ref, blocks, rows=slice(None)):
        return jnp.concatenate([ref[n, rows] for n in blocks], axis=1)

    def geometry(entry, tile):
        _, _, recv_at, send_at, code = places(entry)
        shifts = (
            (code // 3 - 1).astype(F32) * box_side,
            (code % 3 - 1).astype(F32) * box_side,
            (recv_at[0] - 1).astype(F32) * brick_height,
        )
        square = soften
        for axis in range(3):
            recv = recv_wide[recv_at[0], recv_at[1], axis * rows + recv_at[2]]
            send = send_wide[send_at[0], send_at[1], pl.ds(axis * rows + send_at[2], 1), :]
            disp = recv + shifts[axis] - send
            geo_buf[tile, axis] = disp
            square = square + disp * disp
        dist = jnp.sqrt(square)
        inside = dist < jnp.where(entry < count, cutoff_radius, 0.0)
        angle = (0.5 * math.pi / cutoff_radius) * (cutoff_radius - dist)
        square = angle * angle
        sine = angle * poly(square, SIN)
        cosine = poly(square, COS)
        geo_buf[tile, 3] = jnp.where(inside, (-math.pi / cutoff_radius) * sine * cosine, 0.0)
        geo_buf[tile, 4] = 1.0 / dist
        geo_buf[tile, 5] = dist
        geo_buf[tile, 6] = jnp.where(inside, sine * sine, 0.0)

    def geo_row(at, which):
        tile, c = at // per_tile % 2, at % per_tile * 2
        return [geo_buf[tile, which, n : n + 1] for n in (c, c + 1)]

    def basis_stage(at):
        for n, dist in zip(blocks_of(at), geo_row(at, 5)):
            offsets = dist - centres
            basis = jnp.exp(-sharpness * offsets * offsets)
            slant_buf[n] = (-2.0 * sharpness) * basis * offsets
            basis_buf[n] = jnp.concatenate([basis.astype(BF16), ones_rows], axis=0)
        half = nn(lhs_x[...], wide(basis_buf, blocks_of(at)))
        half_buf[at % 2 * 2] = half[:, :LANES]
        half_buf[at % 2 * 2 + 1] = half[:, LANES:]

    def soft_stage(at, entry):
        tower_tile, plate_tile = places(entry)[:2]
        c = at % per_tile * 2
        for n, block in enumerate(blocks_of(at)):
            env_rows = jnp.broadcast_to(geo_row(at, 6)[n], (PART, LANES))
            half_env = 0.5 * env_rows
            log_env = -math.log(2.0) * env_rows
            stack_buf[block, width:] = env_rows[:16].astype(BF16)
            for r in parts:
                tanh = jnp.tanh(half_buf[at % 2 * 2 + n, r])
                soft = jnp.log2(1.0 - tanh)
                soft_buf[block, r] = soft
                stack_buf[block, r] = (soft * log_env).astype(BF16)
                gate_buf[block, r] = (tanh + 1.0) * half_env
                pair = adj_wide[tower_tile, c + n, r] * feat_wide[plate_tile, r]
                pair_buf[block, r] = pair.astype(BF16)

    def product_stage(at):
        blocks = blocks_of(at)
        back = nn(lhs_a[...], wide(pair_buf, blocks))
        lhs = jnp.concatenate([lhs_f[0], lhs_f[1, :, :16]], axis=1)
        filt = nn(lhs, wide(stack_buf, blocks))
        for n in range(2):
            back_buf[at % 2 * 2 + n] = back[:, n * LANES : (n + 1) * LANES]
            filt_buf[at % 2 * 2 + n] = filt[:, n * LANES : (n + 1) * LANES]

    def feature_stage(at, entry):
        tower_tile, plate_tile = places(entry)[:2]
        c = at % per_tile * 2
        for r in parts:
            total = grad_feat[plate_tile, r]
            for n, block in enumerate(blocks_of(at)):
                back = back_buf[at % 2 * 2 + n, r]
                low = slice(width + r.start, width + r.stop)
                both_buf[block, r] = (back * gate_buf[block, r]).astype(BF16)
                both_buf[block, low] = (back * soft_buf[block, r]).astype(BF16)
                total = total + filt_buf[at % 2 * 2 + n, r] * adj_wide[tower_tile, c + n, r]
            grad_feat[plate_tile, r] = total
        for n, block in enumerate(blocks_of(at)):
            inner_buf[block] = back_buf[at % 2 * 2 + n, width : width + 8]

    def radial_stage(at, entry):
        tile, c = at // per_tile % 2, at % per_tile * 2
        lhs = jnp.concatenate([lhs_d[0], lhs_d[1]], axis=1)
        d_basis = nn(lhs, wide(both_buf, blocks_of(at)))
        for n, block in enumerate(blocks_of(at)):
            part = d_basis[:, n * LANES : (n + 1) * LANES]
            direct = jnp.sum(part[:nbasis] * slant_buf[block], axis=0, keepdims=True)
            inner = jnp.sum(inner_buf[block], axis=0, keepdims=True)
            inner = inner - math.log(2.0) * part[nbasis : nbasis + 1]
            pull_buf[c + n : c + n + 1] = direct + geo_row(at, 3)[n] * inner
        whole = blocks_of(at)
        acc_wf[...] += nt(wide(stack_buf, whole), wide(pair_buf, whole))
        acc_wr[...] += nt(wide(basis_buf, whole), wide(both_buf, whole, slice(0, width)))
        if at % per_tile < per_tile - 1:
            return
        _, _, recv_at, send_at, _ = places(entry)
        radial = pull_buf[...] * geo_buf[tile, 4]
        for axis in range(3):
            pull = geo_buf[tile, axis] * radial
            grad_recv[recv_at[0], recv_at[1], axis * rows + recv_at[2]] += pull
            grad_send[send_at[0], send_at[1], axis * rows + send_at[2]] += pull

    parts = [slice(r, r + PART) for r in range(0, width, PART)]
    for ref in (soft_buf, gate_buf):
        ref[2 * ring - 2 :] = jnp.zeros((2, *ref.shape[1:]), ref.dtype)
    for ref in (basis_buf, slant_buf, stack_buf, pair_buf, both_buf, inner_buf):
        ref[2 * ring - 4 :] = jnp.zeros((4, *ref.shape[1:]), ref.dtype)
    for ref in (back_buf, filt_buf, pull_buf):
        ref[...] = jnp.zeros_like(ref)
    geo_buf[1] = jnp.zeros(geo_buf.shape[1:], F32)
    geometry(0, 0)
    basis_stage(0)
    soft_stage(0, 0)
    basis_stage(1)

    def visit(step, carry):
        def entry_of(at):
            return jnp.maximum(TILES * step + at // per_tile, 0)

        for at in range(TILES * per_tile):
            radial_stage(at - 2, entry_of(at - 2))
            feature_stage(at - 1, entry_of(at - 1))
            if at % per_tile == 1:
                geometry(entry_of(at) + 1, (at // per_tile + 1) % 2)
            product_stage(at)
            soft_stage(at + 1, entry_of(at + 1))
            basis_stage(at + 2)
        return carry

    steps = (count + TILES - 1) // TILES
    lax.fori_loop(0, steps, visit, 0)
    last = TILES * steps - 1
    radial_stage(-2, last)
    feature_stage(-1, last)
    radial_stage(-1, last)

    digit = iota((1, width), 1)
    count_row = jnp.where(digit == 0, lax.rem(count, 16), 0)
    count_row = jnp.where(digit == 1, count // 16, count_row).astype(F32)
    weights = jnp.concatenate(
        [
            acc_wf[:width],
            acc_wr[:nbasis],
            acc_wf[width : width + 1],
            acc_wr[nbasis : nbasis + 1],
            count_row,
            jnp.zeros((weight_out.shape[0] - width - nbasis - 3, width), F32),
        ],
        axis=0,
    )
    weight_out[...] = weights
    put_split(send_out, weights)

    fold = one_hot(iota((TILE, LANES), 0) == iota((TILE, LANES), 1) % TILE)
    same_slot = one_hot(iota((LANES, LANES), 0) % TILE == iota((LANES, LANES), 1) % TILE)
    same_group = one_hot(iota((LANES, LANES), 0) // TILE == iota((LANES, LANES), 1) % groups)
    group_of = iota((spots, LANES), 1) // TILE
    padding = jnp.zeros((block_rows - atoms - spots, LANES), F32)
    for step in range(plate_count):
        brick = plate_at ^ step
        at = step // 2 * block_rows
        target = send_out if step % 2 else keep_out
        kind = target.dtype

        def fold_feat(half, carry, brick=brick, at=at, target=target, kind=kind):
            for t in range(per_brick):
                pieces = split(grad_feat[brick * per_brick + t], 2)
                start = pl.multiple_of(at + t * TILE, 16)
                target[pl.ds(start, TILE), :] = (
                    nt(fold, pieces[0]) + nt(fold, pieces[1])
                ).astype(kind)
            return carry

        lax.fori_loop(0, 1, fold_feat, 0)
        total = jnp.zeros((spots, LANES), F32)
        for q in range(groups):
            summed = nn_split(jnp.sum(grad_send[brick, q], axis=1), same_slot)
            total = jnp.where(group_of == q, -summed, total)
        total = jnp.concatenate([total, padding], axis=0)
        target[at + atoms : at + block_rows] = total.astype(kind)
    lane = iota((chunks, LANES), 1)
    own_chunk = (lane // groups) % chunks == iota((chunks, LANES), 0)
    for target, slot in ((far_out, far_slot), (None, 1), (near_out, near_slot)):
        total = jnp.zeros((spots, chunks, LANES), F32)
        for q in range(groups):
            summed = nn_split(grad_recv[slot, q].reshape(spots * chunks, LANES), same_group)
            chosen = own_chunk & (lane // TILE == q)
            total = total + jnp.where(chosen[None], summed.reshape(spots, chunks, LANES), 0.0)
        total = jnp.concatenate([jnp.sum(total, axis=1), padding], axis=0)
        if target is None:
            keep_out[atoms:block_rows] += total
        else:
            target[...] = total


def put_split(target, weights):
    count = weights.shape[0]
    end = target.shape[0]
    high, low = split(weights, 2)
    target[end - 2 * count : end - count] = high
    target[end - count :] = low


def add_kernel(cut, kept_ref, weight_ref, got_ref, near_ref, kept_out, send_out, weight_out):
    held, count = kept_ref.shape[0], weight_out.shape[0] - near_ref.shape[0]
    got = got_ref[...].astype(F32)
    total = kept_ref[...] + got[:held]
    weights = weight_ref[:count] + got[held : held + count] + got[held + count :]
    kept_out[...] = total[:cut]
    send_out[: held - cut] = total[cut:].astype(BF16)
    put_split(send_out, weights)
    weight_out[:count] = weights
    weight_out[count:] = near_ref[...]


def finish_kernel(atoms, count_ref, block_ref, got_ref, near_ref, far_ref, feat_out, pos_out):
    block, width = block_ref.shape
    live = iota((atoms, width), 0) < count_ref[0, 0]
    total = block_ref[...] + got_ref[:block].astype(F32)
    feat_out[0] = jnp.where(live, total[:atoms], 0.0)
    spots = total[atoms:] + near_ref[near_ref.shape[0] - block + atoms :] + far_ref[...]
    rows = atoms // LANES
    for axis in range(3):
        for r in range(rows):
            at = axis * rows + r
            pos_out[axis, :, r * LANES : (r + 1) * LANES] = spots[at : at + 1]


def weight_kernel(*refs):
    ins, outs = refs[:-4], refs[-4:]
    total = ins[0][...]
    for other in ins[1:]:
        total = total + other[...]
    nbasis, width = outs[0].shape
    row = total[width + nbasis + 2 : width + nbasis + 3]
    tiles = row[:, :1] + 16.0 * row[:, 1:2]
    scale = lax.rsqrt(tiles * (TILE * TILE))
    outs[0][...] = total[width : width + nbasis] * scale
    outs[1][...] = total[width + nbasis + 1 : width + nbasis + 2] * scale
    outs[2][...] = total[:width] * scale
    outs[3][...] = total[width + nbasis : width + nbasis + 1] * scale


def swap(value, axis, route):
    size = lax.axis_size(axis)
    return lax.ppermute(value, axis, [(i, route(i) % size) for i in range(size)])


def across(bits):
    return lambda i: i ^ bits


def beyond(i):
    return i + 1 if i % 2 else i - 1


VMEM = pl.BlockSpec(memory_space=pltpu.VMEM)
SMEM = pl.BlockSpec(memory_space=pltpu.SMEM)


def call(kernel, shapes, places, **extra):
    return pl.pallas_call(
        kernel,
        out_shape=[jax.ShapeDtypeStruct(shape, kind) for shape, kind in shapes],
        in_specs=places,
        out_specs=[VMEM] * len(shapes),
        **extra,
    )


def local(
    features,
    adjoint,
    positions,
    w_rbf,
    b_rbf,
    w_filter,
    b_filter,
    atom_counts,
    tile_counts,
    tower_tiles,
    plate_tiles,
    image_shifts,
):
    atoms, width = features.shape[1:]
    nbasis = w_rbf.shape[0]
    per_brick = atoms // TILE
    groups = LANES // TILE
    chunks = TILE // groups
    plate_count = lax.axis_size("plate")
    tower_count = lax.axis_size("tower")
    if min(plate_count // 4, tower_count // 2) < 1 or any(
        size & (size - 1) for size in (plate_count, tower_count)
    ):
        raise ValueError("axis sizes")
    spots = 3 * (atoms // LANES)
    spot_rows = up(spots, 16)
    block = atoms + spot_rows
    weight_rows = up(width + nbasis + 3, 16)

    feat_block, adj_block = call(
        pack_kernel, [((block, width), BF16)] * 2, [SMEM, VMEM, VMEM, VMEM]
    )(atom_counts, features, adjoint, positions.reshape(3, atoms))
    peers = [swap(feat_block, "plate", across(step)) for step in range(1, plate_count)]
    near_adj = swap(adj_block, "tower", across(1))
    far_adj = swap(adj_block, "tower", beyond)

    at = jnp.stack([lax.axis_index("tower"), lax.axis_index("plate")]).astype(jnp.int32)
    half = plate_count // 2
    keep, send, weights, near_pos, far_pos = call(
        functools.partial(tile_kernel, plate_count),
        [
            ((half * block, width), F32),
            ((half * block + 2 * weight_rows, width), BF16),
            ((weight_rows, width), F32),
            ((spot_rows, width), F32),
            ((spot_rows, width), F32),
        ],
        [SMEM] * 5 + [VMEM] * (3 + plate_count + 4),
        scratch_shapes=[
            pltpu.VMEM((3 * per_brick, chunks, width, LANES), F32),
            pltpu.VMEM((plate_count * per_brick, width, LANES), F32),
            pltpu.VMEM((3, groups, spots, chunks, LANES), F32),
            pltpu.VMEM((plate_count, groups, spot_rows, LANES), F32),
            pltpu.VMEM((plate_count * per_brick, width, LANES), F32),
            pltpu.VMEM((3, groups, spots, chunks, LANES), F32),
            pltpu.VMEM((plate_count, groups, spots, chunks, LANES), F32),
            pltpu.VMEM((width + 16, width), F32),
            pltpu.VMEM((2 * nbasis, width), F32),
            pltpu.VMEM((width, 2 * nbasis), BF16),
            pltpu.VMEM((2, width, width), BF16),
            pltpu.VMEM((width + 16, width), BF16),
            pltpu.VMEM((2, 2 * nbasis, width), BF16),
        ]
        + [
            pltpu.VMEM((2 * chunks, width + 16, LANES), BF16),
            pltpu.VMEM((2 * chunks, width, LANES), F32),
            pltpu.VMEM((2 * chunks, width, LANES), F32),
            pltpu.VMEM((2 * chunks, width, LANES), BF16),
            pltpu.VMEM((2 * chunks, 2 * width, LANES), BF16),
            pltpu.VMEM((2 * chunks, 2 * nbasis, LANES), BF16),
            pltpu.VMEM((2 * chunks, nbasis, LANES), F32),
            pltpu.VMEM((2 * chunks, 8, LANES), F32),
            pltpu.VMEM((2, 7, chunks, LANES), F32),
            pltpu.VMEM((chunks, LANES), F32),
            pltpu.VMEM((4, width, LANES), F32),
            pltpu.VMEM((4, width + 16, LANES), F32),
            pltpu.VMEM((4, width, LANES), F32),
        ],
    )(
        at,
        tile_counts,
        tower_tiles,
        plate_tiles,
        image_shifts,
        adj_block,
        near_adj,
        far_adj,
        feat_block,
        *peers,
        w_rbf,
        b_rbf[None],
        w_filter,
        b_filter[None],
    )

    got_far = swap(far_pos, "tower", beyond)
    for step in [1] + [1 << n for n in range(plate_count.bit_length() - 2, 1, -1)]:
        got = swap(send, "plate", across(step))
        held = keep.shape[0]
        cut = held // 2
        keep, send, weights = call(
            functools.partial(add_kernel, cut),
            [
                ((cut, width), F32),
                ((held - cut + 2 * weight_rows, width), BF16),
                ((weight_rows + spot_rows, width), F32),
            ],
            [VMEM] * 4,
        )(keep, weights, got, near_pos)
    both = swap(weights, ("tower", "plate"), across(plate_count + 2))
    near = swap(weights, "tower", across(1))
    got = swap(send, "plate", across(2))
    high, low = (got[-n * weight_rows :][:weight_rows].astype(F32) for n in (2, 1))
    weights = weights[:weight_rows] + high + low
    weights = weights + (near[:weight_rows] + both[:weight_rows])

    bits = 2
    parts = [weights]
    while bits < tower_count:
        weights = sum(parts[1:], parts[0])
        stride = [s * bits for s in (1, 2, 3) if s * bits < tower_count]
        parts = [weights] + [swap(weights, "tower", across(s)) for s in stride]
        bits *= 4
    grad_features, grad_positions = call(
        functools.partial(finish_kernel, atoms),
        [((1, atoms, width), F32), ((3, 1, atoms), F32)],
        [SMEM] + [VMEM] * 4,
    )(atom_counts, keep, got, near, got_far)
    out_wr, out_br, out_wf, out_bf = call(
        weight_kernel,
        [((nbasis, width), F32), ((1, width), F32), ((width, width), F32), ((1, width), F32)],
        [VMEM] * len(parts),
    )(*parts)
    return grad_features, grad_positions, out_wr, out_br[0], out_wf, out_bf[0]


def solution(mesh):
    in_specs = (
        P("tower", "plate", None),
        P("tower", "plate", None),
        P(None, "tower", "plate"),
        P(),
        P(),
        P(),
        P(),
        P("tower", "plate"),
        P("tower", "plate"),
        P("tower", "plate", None),
        P("tower", "plate", None),
        P("tower", "plate", None),
    )
    out_specs = (P("tower", "plate", None), P(None, "tower", "plate"), P(), P(), P(), P())
    return jax.shard_map(local, mesh=mesh, in_specs=in_specs, out_specs=out_specs, check_vma=False)
```

```python
import functools
import math

import jax
import jax.numpy as jnp
from jax import lax
from jax.experimental import pallas as pl
from jax.experimental.pallas import tpu as pltpu
from jax.sharding import PartitionSpec as P


TILE = 32
LANES = 128
PART = 32
TILES = 8

box_side = 1.0
brick_height = 1.0
cutoff_radius = 3.0
soften = 0.01
sharpness = 10.0

F32 = jnp.float32
BF16 = jnp.bfloat16


def up(value, unit):
    return -(-value // unit) * unit


def iota(shape, axis):
    return lax.broadcasted_iota(jnp.int32, shape, axis)


def one_hot(cond):
    return jnp.where(cond, 1.0, 0.0).astype(BF16)


def nn(left, right):
    return lax.dot_general(left, right, (((1,), (0,)), ((), ())), preferred_element_type=F32)


def nt(left, right):
    return lax.dot_general(left, right, (((1,), (1,)), ((), ())), preferred_element_type=F32)


def split(value, parts):
    pieces = []
    for _ in range(parts):
        piece = value.astype(BF16)
        pieces.append(piece)
        value = value - piece.astype(F32)
    return pieces


def nn_split(left, right):
    pieces = split(left, 2)
    return nn(pieces[0], right) + nn(pieces[1], right)


def poly(square, coefs):
    total = jnp.full_like(square, coefs[-1])
    for coef in coefs[-2::-1]:
        total = total * square + coef
    return total


SIN = [(-1.0) ** n / math.factorial(2 * n + 1) for n in range(7)]
COS = [(-1.0) ** n / math.factorial(2 * n) for n in range(8)]


def pack_kernel(count_ref, feat_ref, adj_ref, pos_ref, out_feat, out_adj):
    atoms, width = feat_ref.shape[1:]
    live = iota((atoms, width), 0) < count_ref[0, 0]
    rows = atoms // LANES
    extra = out_feat.shape[0] - atoms
    spots = pos_ref[...].astype(F32)
    parts = [
        spots[axis : axis + 1, r * LANES : (r + 1) * LANES]
        for axis in range(3)
        for r in range(rows)
    ]
    parts.append(jnp.zeros((extra - len(parts), width), F32))
    tail = jnp.concatenate(parts, axis=0).astype(BF16)
    for source, target in ((feat_ref, out_feat), (adj_ref, out_adj)):
        kept = jnp.where(live, source[0].astype(F32), 0.0)
        target[:atoms] = kept.astype(BF16)
        target[atoms:] = tail


def tile_kernel(
    plate_count,
    where_ref,
    count_ref,
    tower_ref,
    plate_ref,
    shift_ref,
    *refs,
):
    (own_adj, near_adj, far_adj), refs = refs[:3], refs[3:]
    feats, refs = refs[:plate_count], refs[plate_count:]
    (w_rbf_ref, b_rbf_ref, w_filter_ref, b_filter_ref), refs = refs[:4], refs[4:]
    (keep_out, send_out, weight_out, near_out, far_out), refs = refs[:5], refs[5:]
    (
        adj_wide,
        feat_wide,
        recv_wide,
        send_wide,
        grad_feat,
        grad_recv,
        grad_send,
        acc_wf,
        acc_wr,
        lhs_x,
        lhs_f,
        lhs_a,
        lhs_d,
    ), refs = refs[:13], refs[13:]
    stack_buf, soft_buf, gate_buf, pair_buf, d_pre_buf, refs = *refs[:5], refs[5:]
    basis_buf, slant_buf, inner_buf, geo_buf, pull_buf, *refs = refs
    half_buf, back_buf, filt_buf = refs
    width = w_filter_ref.shape[0]
    nbasis = w_rbf_ref.shape[0]
    block_rows = own_adj.shape[0]
    groups = LANES // TILE
    chunks = TILE // groups
    pairs = TILE * TILE
    per_brick = adj_wide.shape[0] // 3
    atoms = per_brick * TILE
    rows = atoms // LANES
    spots = 3 * rows
    tower_at = where_ref[0]
    plate_at = where_ref[1]
    odd = lax.rem(tower_at, 2)
    near_slot = 2 - 2 * odd
    far_slot = 2 * odd
    sources = ((far_adj, far_slot), (own_adj, 1), (near_adj, near_slot))

    pick_send = one_hot(iota((TILE, LANES), 0) == iota((TILE, LANES), 1) % TILE)
    for source, slot in sources:
        for half in range(rows):
            turned = source[half * LANES : (half + 1) * LANES].astype(F32).T
            for q in range(groups):
                for c in range(chunks):
                    lane = q * TILE + c * groups + iota((width, LANES), 1) // TILE
                    adj_wide[slot * per_brick + half * groups + q, c] = jnp.take_along_axis(
                        turned, lane, axis=1
                    )
    for q in range(groups):
        pick = one_hot(iota((LANES, pairs), 0) == q * TILE + iota((LANES, pairs), 1) // TILE)
        for source, slot in sources:
            wide = nn(source[atoms:block_rows], pick)
            for c in range(chunks):
                recv_wide[slot, q, :, c, :] = wide[:spots, c * LANES : (c + 1) * LANES]
    for q in range(groups):
        pick = one_hot(iota((LANES, LANES), 0) == q * TILE + iota((LANES, LANES), 1) % TILE)
        for step, source in enumerate(feats):
            send_wide[plate_at ^ step, q] = nn(source[atoms:block_rows], pick)
    for step, source in enumerate(feats):
        brick = plate_at ^ step

        def widen_feat(half, carry, source=source, brick=brick):
            for t in range(per_brick):
                start = pl.multiple_of(t * TILE, TILE)
                part = source[pl.ds(start, TILE), :].astype(F32).T.astype(BF16)
                feat_wide[brick * per_brick + t] = nn(part, pick_send)
            return carry

        lax.fori_loop(0, 1, widen_feat, 0)

    w_rbf = w_rbf_ref[...].astype(F32)
    half_bias = [piece.astype(F32) for piece in split(0.5 * b_rbf_ref[...], 3)]
    stacked = jnp.concatenate(
        [0.5 * w_rbf] + half_bias + [jnp.zeros((LANES - nbasis - 3, width), F32)], axis=0
    )
    lhs_x[...] = stacked.T[:, : 2 * nbasis].astype(BF16)
    w_filter = w_filter_ref[...].astype(F32)
    bias = [piece.astype(F32) for piece in split(b_filter_ref[...], 3)]
    bias = jnp.concatenate(bias + [jnp.zeros((LANES - 3, width), F32)], axis=0)
    lhs_f[0] = w_filter.T.astype(BF16)
    lhs_f[1] = bias.T.astype(BF16)
    lhs_a[:width] = w_filter_ref[...]
    lhs_a[width:] = bias[:16].astype(BF16)
    lhs_d[...] = w_rbf_ref[...]

    grad_feat[...] = jnp.zeros_like(grad_feat)
    grad_recv[...] = jnp.zeros_like(grad_recv)
    grad_send[...] = jnp.zeros_like(grad_send)
    acc_wf[...] = jnp.zeros_like(acc_wf)
    acc_wr[...] = jnp.zeros_like(acc_wr)

    count = count_ref[0, 0]
    span = 2 * LANES
    centres = iota((nbasis, LANES), 0).astype(F32) * (cutoff_radius / (nbasis - 1))
    ones_rows = jnp.ones((nbasis, LANES), BF16)

    def places(entry):
        entry = jnp.minimum(entry, count - 1)
        tower_tile = tower_ref[0, 0, entry]
        plate_tile = plate_ref[0, 0, entry]
        recv_t = tower_tile % per_brick
        send_t = plate_tile % per_brick
        recv = (tower_tile // per_brick, recv_t % groups, recv_t // groups)
        send = (plate_tile // per_brick, send_t % groups, send_t // groups)
        return tower_tile, plate_tile, recv, send, shift_ref[0, 0, entry]

    per_tile = pairs // span
    ring = 2 * per_tile

    def blocks_of(at):
        return (at % ring * 2, at % ring * 2 + 1)

    def wide(ref, blocks, rows=slice(None)):
        return jnp.concatenate([ref[n, rows] for n in blocks], axis=1)

    def geometry(entry, tile):
        _, _, recv_at, send_at, code = places(entry)
        shifts = (
            (code // 3 - 1).astype(F32) * box_side,
            (code % 3 - 1).astype(F32) * box_side,
            (recv_at[0] - 1).astype(F32) * brick_height,
        )
        square = soften
        for axis in range(3):
            recv = recv_wide[recv_at[0], recv_at[1], axis * rows + recv_at[2]]
            send = send_wide[send_at[0], send_at[1], pl.ds(axis * rows + send_at[2], 1), :]
            disp = recv + shifts[axis] - send
            geo_buf[tile, axis] = disp
            square = square + disp * disp
        dist = jnp.sqrt(square)
        inside = dist < jnp.where(entry < count, cutoff_radius, 0.0)
        angle = (0.5 * math.pi / cutoff_radius) * (cutoff_radius - dist)
        square = angle * angle
        sine = angle * poly(square, SIN)
        cosine = poly(square, COS)
        geo_buf[tile, 3] = jnp.where(inside, (-math.pi / cutoff_radius) * sine * cosine, 0.0)
        geo_buf[tile, 4] = 1.0 / dist
        geo_buf[tile, 5] = dist
        geo_buf[tile, 6] = jnp.where(inside, sine * sine, 0.0)

    def geo_row(at, which):
        tile, c = at // per_tile % 2, at % per_tile * 2
        return [geo_buf[tile, which, n : n + 1] for n in (c, c + 1)]

    def basis_stage(at):
        for n, dist in zip(blocks_of(at), geo_row(at, 5)):
            offsets = dist - centres
            basis = jnp.exp(-sharpness * offsets * offsets)
            slant_buf[n] = (-2.0 * sharpness) * basis * offsets
            basis_buf[n] = jnp.concatenate([basis.astype(BF16), ones_rows], axis=0)
        half = nn(lhs_x[...], wide(basis_buf, blocks_of(at)))
        half_buf[at % 2 * 2] = half[:, :LANES]
        half_buf[at % 2 * 2 + 1] = half[:, LANES:]

    def soft_stage(at, entry):
        tower_tile, plate_tile = places(entry)[:2]
        c = at % per_tile * 2
        for n, block in enumerate(blocks_of(at)):
            env_rows = jnp.broadcast_to(geo_row(at, 6)[n], (PART, LANES))
            half_env = 0.5 * env_rows
            log_env = -math.log(2.0) * env_rows
            stack_buf[block, width:] = env_rows[:16].astype(BF16)
            for r in parts:
                tanh = jnp.tanh(half_buf[at % 2 * 2 + n, r])
                soft = jnp.log2(1.0 - tanh)
                soft_buf[block, r] = soft
                stack_buf[block, r] = (soft * log_env).astype(BF16)
                gate_buf[block, r] = (tanh + 1.0) * half_env
                pair = adj_wide[tower_tile, c + n, r] * feat_wide[plate_tile, r]
                pair_buf[block, r] = pair.astype(BF16)

    def product_stage(at):
        blocks = blocks_of(at)
        back = nn(lhs_a[...], wide(pair_buf, blocks))
        lhs = jnp.concatenate([lhs_f[0], lhs_f[1, :, :16]], axis=1)
        filt = nn(lhs, wide(stack_buf, blocks))
        for n in range(2):
            back_buf[at % 2 * 2 + n] = back[:, n * LANES : (n + 1) * LANES]
            filt_buf[at % 2 * 2 + n] = filt[:, n * LANES : (n + 1) * LANES]

    def feature_stage(at, entry):
        tower_tile, plate_tile = places(entry)[:2]
        c = at % per_tile * 2
        inner = [None, None]
        for r in parts:
            total = grad_feat[plate_tile, r]
            for n, block in enumerate(blocks_of(at)):
                back = back_buf[at % 2 * 2 + n, r]
                d_pre_buf[block, r] = (back * gate_buf[block, r]).astype(BF16)
                part = jnp.sum((back * soft_buf[block, r]).reshape(-1, 8, LANES), axis=0)
                inner[n] = part if inner[n] is None else inner[n] + part
                total = total + filt_buf[at % 2 * 2 + n, r] * adj_wide[tower_tile, c + n, r]
            grad_feat[plate_tile, r] = total
        for n, block in enumerate(blocks_of(at)):
            inner_buf[block] = (
                back_buf[at % 2 * 2 + n, width : width + 8] - math.log(2.0) * inner[n]
            )

    def radial_stage(at, entry):
        tile, c = at // per_tile % 2, at % per_tile * 2
        d_basis = nn(lhs_d[...], wide(d_pre_buf, blocks_of(at)))
        for n, block in enumerate(blocks_of(at)):
            part = d_basis[:, n * LANES : (n + 1) * LANES]
            direct = jnp.sum(part * slant_buf[block], axis=0, keepdims=True)
            inner = jnp.sum(inner_buf[block], axis=0, keepdims=True)
            pull_buf[c + n : c + n + 1] = direct + geo_row(at, 3)[n] * inner
        whole = blocks_of(at)
        acc_wf[...] += nt(wide(stack_buf, whole), wide(pair_buf, whole))
        acc_wr[...] += nt(wide(basis_buf, whole), wide(d_pre_buf, whole))
        if at % per_tile < per_tile - 1:
            return
        _, _, recv_at, send_at, _ = places(entry)
        radial = pull_buf[...] * geo_buf[tile, 4]
        for axis in range(3):
            pull = geo_buf[tile, axis] * radial
            grad_recv[recv_at[0], recv_at[1], axis * rows + recv_at[2]] += pull
            grad_send[send_at[0], send_at[1], axis * rows + send_at[2]] += pull

    parts = [slice(r, r + PART) for r in range(0, width, PART)]
    for ref in (soft_buf, gate_buf):
        ref[2 * ring - 2 :] = jnp.zeros((2, *ref.shape[1:]), ref.dtype)
    for ref in (basis_buf, slant_buf, stack_buf, pair_buf, d_pre_buf, inner_buf):
        ref[2 * ring - 4 :] = jnp.zeros((4, *ref.shape[1:]), ref.dtype)
    for ref in (back_buf, filt_buf, pull_buf):
        ref[...] = jnp.zeros_like(ref)
    geo_buf[1] = jnp.zeros(geo_buf.shape[1:], F32)
    geometry(0, 0)
    basis_stage(0)
    soft_stage(0, 0)
    basis_stage(1)

    def visit(step, carry):
        def entry_of(at):
            return jnp.maximum(TILES * step + at // per_tile, 0)

        for at in range(TILES * per_tile):
            radial_stage(at - 2, entry_of(at - 2))
            feature_stage(at - 1, entry_of(at - 1))
            if at % per_tile == 1:
                geometry(entry_of(at) + 1, (at // per_tile + 1) % 2)
            product_stage(at)
            soft_stage(at + 1, entry_of(at + 1))
            basis_stage(at + 2)
        return carry

    steps = (count + TILES - 1) // TILES
    lax.fori_loop(0, steps, visit, 0)
    last = TILES * steps - 1
    radial_stage(-2, last)
    feature_stage(-1, last)
    radial_stage(-1, last)

    digit = iota((1, width), 1)
    count_row = jnp.where(digit == 0, lax.rem(count, 16), 0)
    count_row = jnp.where(digit == 1, count // 16, count_row).astype(F32)
    weights = jnp.concatenate(
        [
            acc_wf[:width],
            acc_wr[:nbasis],
            acc_wf[width : width + 1],
            acc_wr[nbasis : nbasis + 1],
            count_row,
            jnp.zeros((weight_out.shape[0] - width - nbasis - 3, width), F32),
        ],
        axis=0,
    )
    weight_out[...] = weights
    put_split(send_out, weights)

    fold = one_hot(iota((TILE, LANES), 0) == iota((TILE, LANES), 1) % TILE)
    same_slot = one_hot(iota((LANES, LANES), 0) % TILE == iota((LANES, LANES), 1) % TILE)
    same_group = one_hot(iota((LANES, LANES), 0) // TILE == iota((LANES, LANES), 1) % groups)
    group_of = iota((spots, LANES), 1) // TILE
    padding = jnp.zeros((block_rows - atoms - spots, LANES), F32)
    for step in range(plate_count):
        brick = plate_at ^ step
        at = step // 2 * block_rows
        target = send_out if step % 2 else keep_out
        kind = target.dtype

        def fold_feat(half, carry, brick=brick, at=at, target=target, kind=kind):
            for t in range(per_brick):
                pieces = split(grad_feat[brick * per_brick + t], 2)
                start = pl.multiple_of(at + t * TILE, 16)
                target[pl.ds(start, TILE), :] = (
                    nt(fold, pieces[0]) + nt(fold, pieces[1])
                ).astype(kind)
            return carry

        lax.fori_loop(0, 1, fold_feat, 0)
        total = jnp.zeros((spots, LANES), F32)
        for q in range(groups):
            summed = nn_split(jnp.sum(grad_send[brick, q], axis=1), same_slot)
            total = jnp.where(group_of == q, -summed, total)
        total = jnp.concatenate([total, padding], axis=0)
        target[at + atoms : at + block_rows] = total.astype(kind)
    lane = iota((chunks, LANES), 1)
    own_chunk = (lane // groups) % chunks == iota((chunks, LANES), 0)
    for target, slot in ((far_out, far_slot), (None, 1), (near_out, near_slot)):
        total = jnp.zeros((spots, chunks, LANES), F32)
        for q in range(groups):
            summed = nn_split(grad_recv[slot, q].reshape(spots * chunks, LANES), same_group)
            chosen = own_chunk & (lane // TILE == q)
            total = total + jnp.where(chosen[None], summed.reshape(spots, chunks, LANES), 0.0)
        total = jnp.concatenate([jnp.sum(total, axis=1), padding], axis=0)
        if target is None:
            keep_out[atoms:block_rows] += total
        else:
            target[...] = total


def put_split(target, weights):
    count = weights.shape[0]
    end = target.shape[0]
    high, low = split(weights, 2)
    target[end - 2 * count : end - count] = high
    target[end - count :] = low


def add_kernel(cut, kept_ref, weight_ref, got_ref, near_ref, kept_out, send_out, weight_out):
    held, count = kept_ref.shape[0], weight_out.shape[0] - near_ref.shape[0]
    got = got_ref[...].astype(F32)
    total = kept_ref[...] + got[:held]
    weights = weight_ref[:count] + got[held : held + count] + got[held + count :]
    kept_out[...] = total[:cut]
    send_out[: held - cut] = total[cut:].astype(BF16)
    put_split(send_out, weights)
    weight_out[:count] = weights
    weight_out[count:] = near_ref[...]


def finish_kernel(atoms, count_ref, block_ref, got_ref, near_ref, far_ref, feat_out, pos_out):
    block, width = block_ref.shape
    live = iota((atoms, width), 0) < count_ref[0, 0]
    total = block_ref[...] + got_ref[:block].astype(F32)
    feat_out[0] = jnp.where(live, total[:atoms], 0.0)
    spots = total[atoms:] + near_ref[near_ref.shape[0] - block + atoms :] + far_ref[...]
    rows = atoms // LANES
    for axis in range(3):
        for r in range(rows):
            at = axis * rows + r
            pos_out[axis, :, r * LANES : (r + 1) * LANES] = spots[at : at + 1]


def weight_kernel(*refs):
    ins, outs = refs[:-4], refs[-4:]
    total = ins[0][...]
    for other in ins[1:]:
        total = total + other[...]
    nbasis, width = outs[0].shape
    row = total[width + nbasis + 2 : width + nbasis + 3]
    tiles = row[:, :1] + 16.0 * row[:, 1:2]
    scale = lax.rsqrt(tiles * (TILE * TILE))
    outs[0][...] = total[width : width + nbasis] * scale
    outs[1][...] = total[width + nbasis + 1 : width + nbasis + 2] * scale
    outs[2][...] = total[:width] * scale
    outs[3][...] = total[width + nbasis : width + nbasis + 1] * scale


def swap(value, axis, route):
    size = lax.axis_size(axis)
    return lax.ppermute(value, axis, [(i, route(i) % size) for i in range(size)])


def across(bits):
    return lambda i: i ^ bits


def beyond(i):
    return i + 1 if i % 2 else i - 1


VMEM = pl.BlockSpec(memory_space=pltpu.VMEM)
SMEM = pl.BlockSpec(memory_space=pltpu.SMEM)


def call(kernel, shapes, places, **extra):
    return pl.pallas_call(
        kernel,
        out_shape=[jax.ShapeDtypeStruct(shape, kind) for shape, kind in shapes],
        in_specs=places,
        out_specs=[VMEM] * len(shapes),
        **extra,
    )


def local(
    features,
    adjoint,
    positions,
    w_rbf,
    b_rbf,
    w_filter,
    b_filter,
    atom_counts,
    tile_counts,
    tower_tiles,
    plate_tiles,
    image_shifts,
):
    atoms, width = features.shape[1:]
    nbasis = w_rbf.shape[0]
    per_brick = atoms // TILE
    groups = LANES // TILE
    chunks = TILE // groups
    plate_count = lax.axis_size("plate")
    tower_count = lax.axis_size("tower")
    if min(plate_count // 4, tower_count // 2) < 1 or any(
        size & (size - 1) for size in (plate_count, tower_count)
    ):
        raise ValueError("axis sizes")
    spots = 3 * (atoms // LANES)
    spot_rows = up(spots, 16)
    block = atoms + spot_rows
    weight_rows = up(width + nbasis + 3, 16)

    feat_block, adj_block = call(
        pack_kernel, [((block, width), BF16)] * 2, [SMEM, VMEM, VMEM, VMEM]
    )(atom_counts, features, adjoint, positions.reshape(3, atoms))
    peers = [swap(feat_block, "plate", across(step)) for step in range(1, plate_count)]
    near_adj = swap(adj_block, "tower", across(1))
    far_adj = swap(adj_block, "tower", beyond)

    at = jnp.stack([lax.axis_index("tower"), lax.axis_index("plate")]).astype(jnp.int32)
    half = plate_count // 2
    keep, send, weights, near_pos, far_pos = call(
        functools.partial(tile_kernel, plate_count),
        [
            ((half * block, width), F32),
            ((half * block + 2 * weight_rows, width), BF16),
            ((weight_rows, width), F32),
            ((spot_rows, width), F32),
            ((spot_rows, width), F32),
        ],
        [SMEM] * 5 + [VMEM] * (3 + plate_count + 4),
        scratch_shapes=[
            pltpu.VMEM((3 * per_brick, chunks, width, LANES), F32),
            pltpu.VMEM((plate_count * per_brick, width, LANES), F32),
            pltpu.VMEM((3, groups, spots, chunks, LANES), F32),
            pltpu.VMEM((plate_count, groups, spot_rows, LANES), F32),
            pltpu.VMEM((plate_count * per_brick, width, LANES), F32),
            pltpu.VMEM((3, groups, spots, chunks, LANES), F32),
            pltpu.VMEM((plate_count, groups, spots, chunks, LANES), F32),
            pltpu.VMEM((width + 16, width), F32),
            pltpu.VMEM((2 * nbasis, width), F32),
            pltpu.VMEM((width, 2 * nbasis), BF16),
            pltpu.VMEM((2, width, width), BF16),
            pltpu.VMEM((width + 16, width), BF16),
            pltpu.VMEM((nbasis, width), BF16),
        ]
        + [
            pltpu.VMEM((2 * chunks, width + 16, LANES), BF16),
            pltpu.VMEM((2 * chunks, width, LANES), F32),
            pltpu.VMEM((2 * chunks, width, LANES), F32),
            pltpu.VMEM((2 * chunks, width, LANES), BF16),
            pltpu.VMEM((2 * chunks, width, LANES), BF16),
            pltpu.VMEM((2 * chunks, 2 * nbasis, LANES), BF16),
            pltpu.VMEM((2 * chunks, nbasis, LANES), F32),
            pltpu.VMEM((2 * chunks, 8, LANES), F32),
            pltpu.VMEM((2, 7, chunks, LANES), F32),
            pltpu.VMEM((chunks, LANES), F32),
            pltpu.VMEM((4, width, LANES), F32),
            pltpu.VMEM((4, width + 16, LANES), F32),
            pltpu.VMEM((4, width, LANES), F32),
        ],
    )(
        at,
        tile_counts,
        tower_tiles,
        plate_tiles,
        image_shifts,
        adj_block,
        near_adj,
        far_adj,
        feat_block,
        *peers,
        w_rbf,
        b_rbf[None],
        w_filter,
        b_filter[None],
    )

    got_far = swap(far_pos, "tower", beyond)
    for step in [1] + [1 << n for n in range(plate_count.bit_length() - 2, 1, -1)]:
        got = swap(send, "plate", across(step))
        held = keep.shape[0]
        cut = held // 2
        keep, send, weights = call(
            functools.partial(add_kernel, cut),
            [
                ((cut, width), F32),
                ((held - cut + 2 * weight_rows, width), BF16),
                ((weight_rows + spot_rows, width), F32),
            ],
            [VMEM] * 4,
        )(keep, weights, got, near_pos)
    both = swap(weights, ("tower", "plate"), across(plate_count + 2))
    near = swap(weights, "tower", across(1))
    got = swap(send, "plate", across(2))
    high, low = (got[-n * weight_rows :][:weight_rows].astype(F32) for n in (2, 1))
    weights = weights[:weight_rows] + high + low
    weights = weights + (near[:weight_rows] + both[:weight_rows])

    bits = 2
    parts = [weights]
    while bits < tower_count:
        weights = sum(parts[1:], parts[0])
        stride = [s * bits for s in (1, 2, 3) if s * bits < tower_count]
        parts = [weights] + [swap(weights, "tower", across(s)) for s in stride]
        bits *= 4
    grad_features, grad_positions = call(
        functools.partial(finish_kernel, atoms),
        [((1, atoms, width), F32), ((3, 1, atoms), F32)],
        [SMEM] + [VMEM] * 4,
    )(atom_counts, keep, got, near, got_far)
    out_wr, out_br, out_wf, out_bf = call(
        weight_kernel,
        [((nbasis, width), F32), ((1, width), F32), ((width, width), F32), ((1, width), F32)],
        [VMEM] * len(parts),
    )(*parts)
    return grad_features, grad_positions, out_wr, out_br[0], out_wf, out_bf[0]


def solution(mesh):
    in_specs = (
        P("tower", "plate", None),
        P("tower", "plate", None),
        P(None, "tower", "plate"),
        P(),
        P(),
        P(),
        P(),
        P("tower", "plate"),
        P("tower", "plate"),
        P("tower", "plate", None),
        P("tower", "plate", None),
        P("tower", "plate", None),
    )
    out_specs = (P("tower", "plate", None), P(None, "tower", "plate"), P(), P(), P(), P())
    return jax.shard_map(local, mesh=mesh, in_specs=in_specs, out_specs=out_specs, check_vma=False)
```

```python
import functools
import math

import jax
import jax.numpy as jnp
from jax import lax
from jax.experimental import pallas as pl
from jax.experimental.pallas import tpu as pltpu
from jax.sharding import PartitionSpec as P


TILE = 32
LANES = 128
PART = 32
TILES = 8

box_side = 1.0
brick_height = 1.0
cutoff_radius = 3.0
soften = 0.01
sharpness = 10.0

F32 = jnp.float32
BF16 = jnp.bfloat16


def up(value, unit):
    return -(-value // unit) * unit


def iota(shape, axis):
    return lax.broadcasted_iota(jnp.int32, shape, axis)


def one_hot(cond):
    return jnp.where(cond, 1.0, 0.0).astype(BF16)


def nn(left, right):
    return lax.dot_general(left, right, (((1,), (0,)), ((), ())), preferred_element_type=F32)


def nt(left, right):
    return lax.dot_general(left, right, (((1,), (1,)), ((), ())), preferred_element_type=F32)


def split(value, parts):
    pieces = []
    for _ in range(parts):
        piece = value.astype(BF16)
        pieces.append(piece)
        value = value - piece.astype(F32)
    return pieces


def nn_split(left, right):
    pieces = split(left, 2)
    return nn(pieces[0], right) + nn(pieces[1], right)


def poly(square, coefs):
    total = jnp.full_like(square, coefs[-1])
    for coef in coefs[-2::-1]:
        total = total * square + coef
    return total


SIN = [(-1.0) ** n / math.factorial(2 * n + 1) for n in range(7)]
COS = [(-1.0) ** n / math.factorial(2 * n) for n in range(8)]


def pack_kernel(count_ref, feat_ref, adj_ref, pos_ref, out_feat, out_adj):
    atoms, width = feat_ref.shape[1:]
    live = iota((atoms, width), 0) < count_ref[0, 0]
    rows = atoms // LANES
    extra = out_feat.shape[0] - atoms
    spots = pos_ref[...].astype(F32)
    parts = [
        spots[axis : axis + 1, r * LANES : (r + 1) * LANES]
        for axis in range(3)
        for r in range(rows)
    ]
    parts.append(jnp.zeros((extra - len(parts), width), F32))
    tail = jnp.concatenate(parts, axis=0).astype(BF16)
    for source, target in ((feat_ref, out_feat), (adj_ref, out_adj)):
        kept = jnp.where(live, source[0].astype(F32), 0.0)
        target[:atoms] = kept.astype(BF16)
        target[atoms:] = tail


def tile_kernel(
    plate_count,
    where_ref,
    count_ref,
    tower_ref,
    plate_ref,
    shift_ref,
    *refs,
):
    (own_adj, near_adj, far_adj), refs = refs[:3], refs[3:]
    feats, refs = refs[:plate_count], refs[plate_count:]
    (w_rbf_ref, b_rbf_ref, w_filter_ref, b_filter_ref), refs = refs[:4], refs[4:]
    (keep_out, send_out, weight_out, near_out, far_out), refs = refs[:5], refs[5:]
    (
        adj_wide,
        feat_wide,
        recv_wide,
        send_wide,
        grad_feat,
        grad_recv,
        grad_send,
        acc_wf,
        acc_wr,
        lhs_x,
        lhs_f,
        lhs_a,
        lhs_d,
    ), refs = refs[:13], refs[13:]
    stack_buf, soft_buf, gate_buf, pair_buf, d_pre_buf, refs = *refs[:5], refs[5:]
    basis_buf, slant_buf, inner_buf, geo_buf, pull_buf, *refs = refs
    half_buf, back_buf, filt_buf = refs
    width = w_filter_ref.shape[0]
    nbasis = w_rbf_ref.shape[0]
    block_rows = own_adj.shape[0]
    groups = LANES // TILE
    chunks = TILE // groups
    pairs = TILE * TILE
    per_brick = adj_wide.shape[0] // 3
    atoms = per_brick * TILE
    rows = atoms // LANES
    spots = 3 * rows
    tower_at = where_ref[0]
    plate_at = where_ref[1]
    odd = lax.rem(tower_at, 2)
    near_slot = 2 - 2 * odd
    far_slot = 2 * odd
    sources = ((far_adj, far_slot), (own_adj, 1), (near_adj, near_slot))

    pick_send = one_hot(iota((TILE, LANES), 0) == iota((TILE, LANES), 1) % TILE)
    for source, slot in sources:
        for half in range(rows):
            turned = source[half * LANES : (half + 1) * LANES].astype(F32).T
            for q in range(groups):
                for c in range(chunks):
                    lane = q * TILE + c * groups + iota((width, LANES), 1) // TILE
                    adj_wide[slot * per_brick + half * groups + q, c] = jnp.take_along_axis(
                        turned, lane, axis=1
                    )
    for q in range(groups):
        pick = one_hot(iota((LANES, pairs), 0) == q * TILE + iota((LANES, pairs), 1) // TILE)
        for source, slot in sources:
            wide = nn(source[atoms:block_rows], pick)
            for c in range(chunks):
                recv_wide[slot, q, :, c, :] = wide[:spots, c * LANES : (c + 1) * LANES]
    for q in range(groups):
        pick = one_hot(iota((LANES, LANES), 0) == q * TILE + iota((LANES, LANES), 1) % TILE)
        for step, source in enumerate(feats):
            send_wide[plate_at ^ step, q] = nn(source[atoms:block_rows], pick)
    for step, source in enumerate(feats):
        brick = plate_at ^ step

        def widen_feat(half, carry, source=source, brick=brick):
            for t in range(per_brick):
                start = pl.multiple_of(t * TILE, TILE)
                part = source[pl.ds(start, TILE), :].astype(F32).T.astype(BF16)
                feat_wide[brick * per_brick + t] = nn(part, pick_send)
            return carry

        lax.fori_loop(0, 1, widen_feat, 0)

    w_rbf = w_rbf_ref[...].astype(F32)
    half_bias = [piece.astype(F32) for piece in split(0.5 * b_rbf_ref[...], 3)]
    stacked = jnp.concatenate(
        [0.5 * w_rbf] + half_bias + [jnp.zeros((LANES - nbasis - 3, width), F32)], axis=0
    )
    lhs_x[...] = stacked.T[:, : 2 * nbasis].astype(BF16)
    w_filter = w_filter_ref[...].astype(F32)
    bias = [piece.astype(F32) for piece in split(b_filter_ref[...], 3)]
    bias = jnp.concatenate(bias + [jnp.zeros((LANES - 3, width), F32)], axis=0)
    lhs_f[0] = w_filter.T.astype(BF16)
    lhs_f[1] = bias.T.astype(BF16)
    lhs_a[:width] = w_filter_ref[...]
    lhs_a[width:] = bias[:16].astype(BF16)
    lhs_d[...] = w_rbf_ref[...]

    grad_feat[...] = jnp.zeros_like(grad_feat)
    grad_recv[...] = jnp.zeros_like(grad_recv)
    grad_send[...] = jnp.zeros_like(grad_send)
    acc_wf[...] = jnp.zeros_like(acc_wf)
    acc_wr[...] = jnp.zeros_like(acc_wr)

    count = count_ref[0, 0]
    span = 2 * LANES
    centres = iota((nbasis, LANES), 0).astype(F32) * (cutoff_radius / (nbasis - 1))
    ones_rows = jnp.ones((nbasis, LANES), BF16)

    def places(entry):
        entry = jnp.minimum(entry, count - 1)
        tower_tile = tower_ref[0, 0, entry]
        plate_tile = plate_ref[0, 0, entry]
        recv_t = tower_tile % per_brick
        send_t = plate_tile % per_brick
        recv = (tower_tile // per_brick, recv_t % groups, recv_t // groups)
        send = (plate_tile // per_brick, send_t % groups, send_t // groups)
        return tower_tile, plate_tile, recv, send, shift_ref[0, 0, entry]

    per_tile = pairs // span
    ring = 2 * per_tile

    def blocks_of(at):
        return (at % ring * 2, at % ring * 2 + 1)

    def wide(ref, blocks, rows=slice(None)):
        return jnp.concatenate([ref[n, rows] for n in blocks], axis=1)

    def geometry(entry, tile):
        _, _, recv_at, send_at, code = places(entry)
        shifts = (
            (code // 3 - 1).astype(F32) * box_side,
            (code % 3 - 1).astype(F32) * box_side,
            (recv_at[0] - 1).astype(F32) * brick_height,
        )
        square = soften
        for axis in range(3):
            recv = recv_wide[recv_at[0], recv_at[1], axis * rows + recv_at[2]]
            send = send_wide[send_at[0], send_at[1], pl.ds(axis * rows + send_at[2], 1), :]
            disp = recv + shifts[axis] - send
            geo_buf[tile, axis] = disp
            square = square + disp * disp
        dist = jnp.sqrt(square)
        inside = dist < jnp.where(entry < count, cutoff_radius, 0.0)
        angle = (0.5 * math.pi / cutoff_radius) * (cutoff_radius - dist)
        square = angle * angle
        sine = angle * poly(square, SIN)
        cosine = poly(square, COS)
        geo_buf[tile, 3] = jnp.where(inside, (-math.pi / cutoff_radius) * sine * cosine, 0.0)
        geo_buf[tile, 4] = 1.0 / dist
        geo_buf[tile, 5] = dist
        geo_buf[tile, 6] = jnp.where(inside, sine * sine, 0.0)

    def geo_row(at, which):
        tile, c = at // per_tile % 2, at % per_tile * 2
        return [geo_buf[tile, which, n : n + 1] for n in (c, c + 1)]

    def basis_stage(at):
        for n, dist in zip(blocks_of(at), geo_row(at, 5)):
            offsets = dist - centres
            basis = jnp.exp(-sharpness * offsets * offsets)
            slant_buf[n] = (-2.0 * sharpness) * basis * offsets
            basis_buf[n] = jnp.concatenate([basis.astype(BF16), ones_rows], axis=0)
        half = nn(lhs_x[...], wide(basis_buf, blocks_of(at)))
        half_buf[at % 2 * 2] = half[:, :LANES]
        half_buf[at % 2 * 2 + 1] = half[:, LANES:]

    def soft_stage(at, entry):
        tower_tile, plate_tile = places(entry)[:2]
        c = at % per_tile * 2
        for n, block in enumerate(blocks_of(at)):
            env_rows = jnp.broadcast_to(geo_row(at, 6)[n], (PART, LANES))
            half_env = 0.5 * env_rows
            log_env = -math.log(2.0) * env_rows
            stack_buf[block, width:] = env_rows[:16].astype(BF16)
            for r in parts:
                tanh = jnp.tanh(half_buf[at % 2 * 2 + n, r])
                soft = jnp.log2(1.0 - tanh)
                soft_buf[block, r] = soft
                stack_buf[block, r] = (soft * log_env).astype(BF16)
                gate_buf[block, r] = (tanh + 1.0) * half_env
                pair = adj_wide[tower_tile, c + n, r] * feat_wide[plate_tile, r]
                pair_buf[block, r] = pair.astype(BF16)

    def product_stage(at):
        blocks = blocks_of(at)
        back = nn(lhs_a[...], wide(pair_buf, blocks))
        lhs = jnp.concatenate([lhs_f[0], lhs_f[1, :, :16]], axis=1)
        filt = nn(lhs, wide(stack_buf, blocks))
        for n in range(2):
            back_buf[at % 2 * 2 + n] = back[:, n * LANES : (n + 1) * LANES]
            filt_buf[at % 2 * 2 + n] = filt[:, n * LANES : (n + 1) * LANES]

    def feature_stage(at, entry):
        tower_tile, plate_tile = places(entry)[:2]
        c = at % per_tile * 2
        inner = [None, None]
        for r in parts:
            total = grad_feat[plate_tile, r]
            for n, block in enumerate(blocks_of(at)):
                back = back_buf[at % 2 * 2 + n, r]
                d_pre_buf[block, r] = (back * gate_buf[block, r]).astype(BF16)
                part = jnp.sum((back * soft_buf[block, r]).reshape(-1, 8, LANES), axis=0)
                inner[n] = part if inner[n] is None else inner[n] + part
                total = total + filt_buf[at % 2 * 2 + n, r] * adj_wide[tower_tile, c + n, r]
            grad_feat[plate_tile, r] = total
        for n, block in enumerate(blocks_of(at)):
            inner_buf[block] = (
                back_buf[at % 2 * 2 + n, width : width + 8] - math.log(2.0) * inner[n]
            )

    def radial_stage(at, entry):
        tile, c = at // per_tile % 2, at % per_tile * 2
        d_basis = nn(lhs_d[...], wide(d_pre_buf, blocks_of(at)))
        for n, block in enumerate(blocks_of(at)):
            part = d_basis[:, n * LANES : (n + 1) * LANES]
            direct = jnp.sum(part * slant_buf[block], axis=0, keepdims=True)
            inner = jnp.sum(inner_buf[block], axis=0, keepdims=True)
            pull_buf[c + n : c + n + 1] = direct + geo_row(at, 3)[n] * inner
        whole = blocks_of(at)
        acc_wf[...] += nt(wide(stack_buf, whole), wide(pair_buf, whole))
        acc_wr[...] += nt(wide(basis_buf, whole), wide(d_pre_buf, whole))
        if at % per_tile < per_tile - 1:
            return
        _, _, recv_at, send_at, _ = places(entry)
        radial = pull_buf[...] * geo_buf[tile, 4]
        for axis in range(3):
            pull = geo_buf[tile, axis] * radial
            grad_recv[recv_at[0], recv_at[1], axis * rows + recv_at[2]] += pull
            grad_send[send_at[0], send_at[1], axis * rows + send_at[2]] += pull

    parts = [slice(r, r + PART) for r in range(0, width, PART)]
    for ref in (soft_buf, gate_buf):
        ref[2 * ring - 2 :] = jnp.zeros((2, *ref.shape[1:]), ref.dtype)
    for ref in (basis_buf, slant_buf, stack_buf, pair_buf, d_pre_buf, inner_buf):
        ref[2 * ring - 4 :] = jnp.zeros((4, *ref.shape[1:]), ref.dtype)
    for ref in (back_buf, filt_buf, pull_buf):
        ref[...] = jnp.zeros_like(ref)
    geo_buf[1] = jnp.zeros(geo_buf.shape[1:], F32)
    geometry(0, 0)
    basis_stage(0)
    soft_stage(0, 0)
    basis_stage(1)

    def visit(step, carry):
        def entry_of(at):
            return jnp.maximum(TILES * step + at // per_tile, 0)

        for at in range(TILES * per_tile):
            radial_stage(at - 2, entry_of(at - 2))
            feature_stage(at - 1, entry_of(at - 1))
            if at % per_tile == 1:
                geometry(entry_of(at) + 1, (at // per_tile + 1) % 2)
            product_stage(at)
            soft_stage(at + 1, entry_of(at + 1))
            basis_stage(at + 2)
        return carry

    steps = (count + TILES - 1) // TILES
    lax.fori_loop(0, steps, visit, 0)
    last = TILES * steps - 1
    radial_stage(-2, last)
    feature_stage(-1, last)
    radial_stage(-1, last)

    digit = jnp.minimum(iota((1, width), 1), 16)
    count_row = jnp.where(digit < 16, (count >> digit) & 1, 0).astype(F32)
    weights = jnp.concatenate(
        [
            acc_wf[:width],
            acc_wr[:nbasis],
            acc_wf[width : width + 1],
            acc_wr[nbasis : nbasis + 1],
            count_row,
            jnp.zeros((weight_out.shape[0] - width - nbasis - 3, width), F32),
        ],
        axis=0,
    )
    weight_out[...] = weights
    put_split(send_out, weights)

    fold = one_hot(iota((TILE, LANES), 0) == iota((TILE, LANES), 1) % TILE)
    same_slot = one_hot(iota((LANES, LANES), 0) % TILE == iota((LANES, LANES), 1) % TILE)
    same_group = one_hot(iota((LANES, LANES), 0) // TILE == iota((LANES, LANES), 1) % groups)
    group_of = iota((spots, LANES), 1) // TILE
    padding = jnp.zeros((block_rows - atoms - spots, LANES), F32)
    for step in range(plate_count):
        brick = plate_at ^ step
        at = step // 2 * block_rows
        target = send_out if step % 2 else keep_out
        kind = target.dtype

        def fold_feat(half, carry, brick=brick, at=at, target=target, kind=kind):
            for t in range(per_brick):
                pieces = split(grad_feat[brick * per_brick + t], 2)
                start = pl.multiple_of(at + t * TILE, 16)
                target[pl.ds(start, TILE), :] = (
                    nt(fold, pieces[0]) + nt(fold, pieces[1])
                ).astype(kind)
            return carry

        lax.fori_loop(0, 1, fold_feat, 0)
        total = jnp.zeros((spots, LANES), F32)
        for q in range(groups):
            summed = nn_split(jnp.sum(grad_send[brick, q], axis=1), same_slot)
            total = jnp.where(group_of == q, -summed, total)
        total = jnp.concatenate([total, padding], axis=0)
        target[at + atoms : at + block_rows] = total.astype(kind)
    lane = iota((chunks, LANES), 1)
    own_chunk = (lane // groups) % chunks == iota((chunks, LANES), 0)
    for target, slot in ((far_out, far_slot), (None, 1), (near_out, near_slot)):
        total = jnp.zeros((spots, chunks, LANES), F32)
        for q in range(groups):
            summed = nn_split(grad_recv[slot, q].reshape(spots * chunks, LANES), same_group)
            chosen = own_chunk & (lane // TILE == q)
            total = total + jnp.where(chosen[None], summed.reshape(spots, chunks, LANES), 0.0)
        total = jnp.concatenate([jnp.sum(total, axis=1), padding], axis=0)
        if target is None:
            keep_out[atoms:block_rows] += total
        else:
            target[...] = total


def put_split(target, weights):
    count = weights.shape[0]
    end = target.shape[0]
    high, low = split(weights, 2)
    target[end - 2 * count : end - count] = high
    target[end - count :] = low


def add_kernel(cut, kept_ref, weight_ref, got_ref, near_ref, kept_out, send_out, weight_out):
    held, count = kept_ref.shape[0], weight_out.shape[0] - near_ref.shape[0]
    got = got_ref[...].astype(F32)
    total = kept_ref[...] + got[:held]
    weights = weight_ref[:count] + got[held : held + count] + got[held + count :]
    kept_out[...] = total[:cut]
    send_out[: held - cut] = total[cut:].astype(BF16)
    put_split(send_out, weights)
    weight_out[:count] = weights
    weight_out[count:] = near_ref[...]


def finish_kernel(atoms, count_ref, block_ref, got_ref, near_ref, far_ref, feat_out, pos_out):
    block, width = block_ref.shape
    live = iota((atoms, width), 0) < count_ref[0, 0]
    total = block_ref[...] + got_ref[:block].astype(F32)
    feat_out[0] = jnp.where(live, total[:atoms], 0.0)
    spots = total[atoms:] + near_ref[near_ref.shape[0] - block + atoms :] + far_ref[...]
    rows = atoms // LANES
    for axis in range(3):
        for r in range(rows):
            at = axis * rows + r
            pos_out[axis, :, r * LANES : (r + 1) * LANES] = spots[at : at + 1]


def weight_kernel(*refs):
    ins, outs = refs[:-4], refs[-4:]
    total = ins[0][...].astype(F32)
    for other in ins[1:]:
        total = total + other[...].astype(F32)
    nbasis, width = outs[0].shape
    row = total[width + nbasis + 2 : width + nbasis + 3]
    digit = jnp.minimum(iota((1, width), 1), 16)
    worth = jnp.where(digit < 16, 1 << digit, 0).astype(F32)
    tiles = jnp.sum(row * worth, axis=1, keepdims=True)
    scale = lax.rsqrt(tiles * (TILE * TILE))
    outs[0][...] = total[width : width + nbasis] * scale
    outs[1][...] = total[width + nbasis + 1 : width + nbasis + 2] * scale
    outs[2][...] = total[:width] * scale
    outs[3][...] = total[width + nbasis : width + nbasis + 1] * scale


def swap(value, axis, route):
    size = lax.axis_size(axis)
    return lax.ppermute(value, axis, [(i, route(i) % size) for i in range(size)])


def across(bits):
    return lambda i: i ^ bits


def beyond(i):
    return i + 1 if i % 2 else i - 1


VMEM = pl.BlockSpec(memory_space=pltpu.VMEM)
SMEM = pl.BlockSpec(memory_space=pltpu.SMEM)


def call(kernel, shapes, places, **extra):
    return pl.pallas_call(
        kernel,
        out_shape=[jax.ShapeDtypeStruct(shape, kind) for shape, kind in shapes],
        in_specs=places,
        out_specs=[VMEM] * len(shapes),
        **extra,
    )


def local(
    features,
    adjoint,
    positions,
    w_rbf,
    b_rbf,
    w_filter,
    b_filter,
    atom_counts,
    tile_counts,
    tower_tiles,
    plate_tiles,
    image_shifts,
):
    atoms, width = features.shape[1:]
    nbasis = w_rbf.shape[0]
    per_brick = atoms // TILE
    groups = LANES // TILE
    chunks = TILE // groups
    plate_count = lax.axis_size("plate")
    tower_count = lax.axis_size("tower")
    if min(plate_count // 4, tower_count // 2) < 1 or any(
        size & (size - 1) for size in (plate_count, tower_count)
    ):
        raise ValueError("axis sizes")
    spots = 3 * (atoms // LANES)
    spot_rows = up(spots, 16)
    block = atoms + spot_rows
    weight_rows = up(width + nbasis + 3, 16)

    feat_block, adj_block = call(
        pack_kernel, [((block, width), BF16)] * 2, [SMEM, VMEM, VMEM, VMEM]
    )(atom_counts, features, adjoint, positions.reshape(3, atoms))
    peers = [swap(feat_block, "plate", across(step)) for step in range(1, plate_count)]
    near_adj = swap(adj_block, "tower", across(1))
    far_adj = swap(adj_block, "tower", beyond)

    at = jnp.stack([lax.axis_index("tower"), lax.axis_index("plate")]).astype(jnp.int32)
    half = plate_count // 2
    keep, send, weights, near_pos, far_pos = call(
        functools.partial(tile_kernel, plate_count),
        [
            ((half * block, width), F32),
            ((half * block + 2 * weight_rows, width), BF16),
            ((weight_rows, width), F32),
            ((spot_rows, width), F32),
            ((spot_rows, width), F32),
        ],
        [SMEM] * 5 + [VMEM] * (3 + plate_count + 4),
        scratch_shapes=[
            pltpu.VMEM((3 * per_brick, chunks, width, LANES), F32),
            pltpu.VMEM((plate_count * per_brick, width, LANES), F32),
            pltpu.VMEM((3, groups, spots, chunks, LANES), F32),
            pltpu.VMEM((plate_count, groups, spot_rows, LANES), F32),
            pltpu.VMEM((plate_count * per_brick, width, LANES), F32),
            pltpu.VMEM((3, groups, spots, chunks, LANES), F32),
            pltpu.VMEM((plate_count, groups, spots, chunks, LANES), F32),
            pltpu.VMEM((width + 16, width), F32),
            pltpu.VMEM((2 * nbasis, width), F32),
            pltpu.VMEM((width, 2 * nbasis), BF16),
            pltpu.VMEM((2, width, width), BF16),
            pltpu.VMEM((width + 16, width), BF16),
            pltpu.VMEM((nbasis, width), BF16),
        ]
        + [
            pltpu.VMEM((2 * chunks, width + 16, LANES), BF16),
            pltpu.VMEM((2 * chunks, width, LANES), F32),
            pltpu.VMEM((2 * chunks, width, LANES), F32),
            pltpu.VMEM((2 * chunks, width, LANES), BF16),
            pltpu.VMEM((2 * chunks, width, LANES), BF16),
            pltpu.VMEM((2 * chunks, 2 * nbasis, LANES), BF16),
            pltpu.VMEM((2 * chunks, nbasis, LANES), F32),
            pltpu.VMEM((2 * chunks, 8, LANES), F32),
            pltpu.VMEM((2, 7, chunks, LANES), F32),
            pltpu.VMEM((chunks, LANES), F32),
            pltpu.VMEM((4, width, LANES), F32),
            pltpu.VMEM((4, width + 16, LANES), F32),
            pltpu.VMEM((4, width, LANES), F32),
        ],
    )(
        at,
        tile_counts,
        tower_tiles,
        plate_tiles,
        image_shifts,
        adj_block,
        near_adj,
        far_adj,
        feat_block,
        *peers,
        w_rbf,
        b_rbf[None],
        w_filter,
        b_filter[None],
    )

    got_far = swap(far_pos, "tower", beyond)
    for step in [1] + [1 << n for n in range(plate_count.bit_length() - 2, 1, -1)]:
        got = swap(send, "plate", across(step))
        held = keep.shape[0]
        cut = held // 2
        keep, send, weights = call(
            functools.partial(add_kernel, cut),
            [
                ((cut, width), F32),
                ((held - cut + 2 * weight_rows, width), BF16),
                ((weight_rows + spot_rows, width), F32),
            ],
            [VMEM] * 4,
        )(keep, weights, got, near_pos)
    both = swap(weights, ("tower", "plate"), across(plate_count + 2))
    near = swap(weights, "tower", across(1))
    got = swap(send, "plate", across(2))
    high, low = (got[-n * weight_rows :][:weight_rows].astype(F32) for n in (2, 1))
    weights = weights[:weight_rows] + high + low
    weights = weights + (near[:weight_rows] + both[:weight_rows])

    bits = 2
    parts = [weights]
    while bits < tower_count:
        weights = sum((part.astype(F32) for part in parts[1:]), parts[0].astype(F32))
        weights = weights.astype(BF16)
        stride = [s * bits for s in (1, 2, 3) if s * bits < tower_count]
        parts = [weights] + [swap(weights, "tower", across(s)) for s in stride]
        bits *= 4
    grad_features, grad_positions = call(
        functools.partial(finish_kernel, atoms),
        [((1, atoms, width), F32), ((3, 1, atoms), F32)],
        [SMEM] + [VMEM] * 4,
    )(atom_counts, keep, got, near, got_far)
    out_wr, out_br, out_wf, out_bf = call(
        weight_kernel,
        [((nbasis, width), F32), ((1, width), F32), ((width, width), F32), ((1, width), F32)],
        [VMEM] * len(parts),
    )(*parts)
    return grad_features, grad_positions, out_wr, out_br[0], out_wf, out_bf[0]


def solution(mesh):
    in_specs = (
        P("tower", "plate", None),
        P("tower", "plate", None),
        P(None, "tower", "plate"),
        P(),
        P(),
        P(),
        P(),
        P("tower", "plate"),
        P("tower", "plate"),
        P("tower", "plate", None),
        P("tower", "plate", None),
        P("tower", "plate", None),
    )
    out_specs = (P("tower", "plate", None), P(None, "tower", "plate"), P(), P(), P(), P())
    return jax.shard_map(local, mesh=mesh, in_specs=in_specs, out_specs=out_specs, check_vma=False)
```
